32 devices in a mesh: groups: 2 (over y), gx: 4 (over z), gy: 2 (over x), vert: 2 (over core).
Axes of the slice: x: 2, y: 2, z: 4, core: 2. Of those that a mesh axis runs over, the one named last changes fastest.
Arguments:
- tiles: bfloat16 [6, 2, 128, 8, 16, 128], P('vert', 'gy', ('groups', 'gx')), parts along dimension 2, may hold values from 0.19921875 to 5
- tile_block: int32 [6, 2, 128, 1], P(None, None, 'groups'), parts along dimension 2, may hold values from 0 to 3; in each aligned block of 16 rows (0 to 15, 16 to 31, ..., all dimensions but the last counted through in order) at most 8 rows name the same one
- tile_x: int32 [6, 2, 128], P(None, None, 'groups'), parts along dimension 2, may hold values from 0 to 24
- tile_y: int32 [6, 2, 128], P(None, None, 'groups'), parts along dimension 2, may hold values from 0 to 48
- psf: float32 [6, 3, 15], replicated, may hold values from 0.03 to 0.1
- initial: float32 [256, 128, 128], P(('groups', 'gx'), 'gy'), parts along dimension 0, may hold values from 0.5 to 2
Outputs:
- estimate: float32 [256, 128, 128], P(('groups', 'gx'), 'gy'), parts along dimension 0
The draws below stay inside these ranges and needn't reach their ends.
There are 2 independent parts, one for each index of `groups`. The reference program is written for one: setup_inputs(seed, part) draws one part's arguments, and reference() takes and returns one part's arrays. A program takes and returns all parts, laid end to end along the dimension named above; an argument that names none is the same for every part. Nothing has to cross between parts.
Inputs may be any that keep to these rules, and one draw needn't show every extreme that they name: `tile_block`: among the 16 tiles of one view held by one device (tile numbers in aligned groups of 16 within a block row), no block column is named more than 8 times.
All inputs are finite; a program needn't handle non-finite values.
Results may differ from the reference program's by a relative error of at most 0.0009.
Values may be sent and summed in bfloat16 or wider, within the bound.
A program may use at most 128 MiB of HBM per device.

```python
import math
import jax
import jax.numpy as jnp
import numpy as np
from jax import lax

VIEWS = 6
TAPS = 15
TX = 8
TY = 16
NZ = 128
BY = 64
ITERS = 2
BX = 32
NX = 128
NY = 128
TILES_DEV = 16
TCOLS = 64
CAP = 8
N_GX = 4
N_GY = 2


def with_ends(result, own_key, least, top_value):
    index_at = [jax.random.randint(jax.random.fold_in(own_key, axis), (), 0, length) for axis, length in enumerate(result.shape)]
    longest = result.shape.index(max(result.shape))
    next_to = index_at[:longest] + [(index_at[longest] + 1) % result.shape[longest]] + index_at[longest + 1:]
    return result.at[tuple(index_at)].set(least).at[tuple(next_to)].set(top_value)


def steps_of(key, dims, cuts, smallest, high):
    def one(axis_at, parts):
        steps = jax.random.uniform(jax.random.fold_in(jax.random.fold_in(key, 6), axis_at), (parts,), jnp.float32, smallest / len(cuts), high / len(cuts))
        return jnp.repeat(jnp.exp(steps), dims[axis_at] // parts).reshape((-1,) + (1,) * (len(dims) - axis_at - 1))

    loudness = one(*cuts[0])
    for cut in cuts[1:]:
        loudness = loudness * one(*cut)
    return loudness


def shared_out(stream_key, own, number, rows, count, top, limit, lean):
    ranking = jax.random.permutation(stream_key, count)
    packed, ordinary = load_shares(count, rows * top, limit, lean, True), load_shares(count, rows * top, limit, lean, False)
    places = jnp.arange(count)

    def named(sizes, turn):
        used = int((sizes > 0).sum())
        fixed = max(1, used // 4)
        passed = fixed + (places - fixed + turn * (used - fixed)) % max(1, count - fixed)
        return jnp.zeros((count,), jnp.int32).at[ranking[jnp.where(places < fixed, places, passed)]].set(jnp.asarray(sizes, jnp.int32))

    sizes = jnp.where(number % 4 == 0, named(packed, number // 4), named(ordinary, number - number // 4 - 1))
    mixed = jax.random.permutation(jax.random.fold_in(own, 3), count)
    donor, taker = mixed[0:count // 2 * 2:2], mixed[1:count // 2 * 2:2]
    room = jnp.minimum(sizes[donor] - 1, limit - sizes[taker]) // 2
    room = jnp.where((donor == ranking[0]) | (taker == ranking[0]) | (sizes[taker] == 0), 0, jnp.maximum(room, 0))
    passed = jax.random.randint(jax.random.fold_in(own, 4), (count // 2,), 0, 1 << 20) % (room + 1)
    sizes = sizes.at[donor].add(-passed).at[taker].add(passed)
    labels = jnp.searchsorted(jnp.cumsum(sizes), jnp.arange(rows * top), side="right").astype(jnp.int32)
    table = labels.reshape(top, rows).T
    table = table[jax.random.permutation(jax.random.fold_in(own, 1), rows)]
    turn = jax.random.randint(jax.random.fold_in(own, 2), (rows, 1), 0, top)
    return jnp.take_along_axis(table, (jnp.arange(top)[None, :] + turn) % top, axis=1)


def load_shares(amount, total, most, skew, full):
    weights = [(1 << 20) // math.isqrt(rank ** skew) + 1 for rank in range(1, amount + 1)]
    largest = most if full else min(most, max(-(-total // amount), total * weights[0] // sum(weights)))
    least = 1 if total - largest >= amount - 1 else 0
    holding, rest = [largest] + [least] * (amount - 1), total - largest - least * (amount - 1)
    while rest > 0:
        free = [i for i in range(1, amount) if holding[i] < largest] or [i for i in range(1, amount) if holding[i] < most]
        mass, remaining = sum([weights[i] for i in free]), rest
        for i in free:
            addition = min(most - holding[i], max(1, remaining * weights[i] // mass), rest)
            holding[i] = holding[i] + addition
            rest = rest - addition
    return np.array(holding)


def setup_inputs(seed: int = 0, part: int = 0) -> dict:
    keys = jax.random.split(jax.random.key(seed), 7)
    part_keys = jax.random.split(jax.random.fold_in(keys[6], part), 7)
    tiles = jnp.clip(jnp.exp(math.log(5.0) - 3.2227897 * jax.random.uniform(part_keys[0], (VIEWS, N_GY, TCOLS, TX, TY, NZ), jnp.float32) ** steps_of(part_keys[0], (VIEWS, N_GY, TCOLS, TX, TY, NZ), ((0, 2), (1, 2), (2, 4)), -0.2, 0.2)), 0.19921875, 5.0).astype(jnp.bfloat16)
    tile_block_keys = jax.random.split(jax.random.fold_in(part_keys[1], 1), VIEWS * N_GY * TCOLS // TILES_DEV)
    tile_block_turns = jax.random.permutation(jax.random.fold_in(part_keys[1], 3), VIEWS * N_GY * TCOLS // TILES_DEV)
    tile_block = jax.vmap(lambda own, number: shared_out(jax.random.fold_in(part_keys[1], 2), own, number, TILES_DEV, N_GX, 1, CAP, 2))(tile_block_keys, tile_block_turns).reshape((VIEWS, N_GY, TCOLS, 1))
    tile_x = with_ends(jax.random.randint(part_keys[2], (VIEWS, N_GY, TCOLS), 0, BX - TX + 1), jax.random.fold_in(part_keys[2], 1), 0, BX - TX).astype(jnp.int32)
    tile_y = with_ends(jax.random.randint(part_keys[3], (VIEWS, N_GY, TCOLS), 0, BY - TY + 1), jax.random.fold_in(part_keys[3], 1), 0, BY - TY).astype(jnp.int32)
    psf = jnp.clip(jax.random.uniform(keys[4], (VIEWS, 3, TAPS), jnp.float32, 0.03, 0.1), 0.03, 0.1)
    initial = jnp.clip(jnp.exp(math.log(2.0) - 1.3862944 * jax.random.uniform(part_keys[5], (NX, NY, NZ), jnp.float32) ** steps_of(part_keys[5], (NX, NY, NZ), ((0, 4), (1, 2)), -0.2, 0.2)), 0.5, 2.0)
    return {"tiles": tiles, "tile_block": tile_block, "tile_x": tile_x, "tile_y": tile_y, "psf": psf, "initial": initial}


soft_floor = 0.01
damping = 0.5


def valid_pass(volume, kernel, dimension, adjoint):
    radius = kernel.shape[0] // 2
    length = volume.shape[dimension] - 2 * radius
    summed = None
    for tap_index in range(kernel.shape[0]):
        offset = 2 * radius - tap_index if adjoint else tap_index
        weighted = kernel[tap_index] * lax.slice_in_dim(volume, offset, offset + length, axis=dimension)
        summed = weighted if summed is None else summed + weighted
    return summed


def padded_pass(volume, kernel, dimension, adjoint):
    radius = kernel.shape[0] // 2
    margins = [(0, 0)] * volume.ndim
    margins[dimension] = (radius, radius)
    return valid_pass(jnp.pad(volume, margins), kernel, dimension, adjoint)


def blur(volume, kernels):
    volume = padded_pass(volume, kernels[0], 0, False)
    volume = padded_pass(volume, kernels[1], 1, False)
    return padded_pass(volume, kernels[2], 2, False)


def back_project(volume, kernels):
    volume = padded_pass(volume, kernels[2], 2, True)
    volume = padded_pass(volume, kernels[0], 0, True)
    return padded_pass(volume, kernels[1], 1, True)


def assemble(view_tiles, view_blocks, view_x, view_y):
    tile_rows = jnp.repeat(jnp.arange(N_GY, dtype=jnp.int32), TCOLS)
    flat_tiles = view_tiles.reshape(N_GY * TCOLS, TX, TY, NZ)
    start_x = (view_blocks.reshape(-1) * BX + view_x.reshape(-1)).astype(jnp.int32)
    start_y = (tile_rows * BY + view_y.reshape(-1)).astype(jnp.int32)

    def deposit(state_pair, scanned):
        summed, counted = state_pair
        tile_piece, corner_x, corner_y = scanned
        anchor = jnp.zeros((), jnp.int32)
        existing = lax.dynamic_slice(summed, (corner_x, corner_y, anchor), (TX, TY, NZ))
        summed = lax.dynamic_update_slice(summed, existing + tile_piece.astype(jnp.float32), (corner_x, corner_y, anchor))
        covered = lax.dynamic_slice(counted, (corner_x, corner_y), (TX, TY))
        counted = lax.dynamic_update_slice(counted, covered + 1.0, (corner_x, corner_y))
        return (summed, counted), None

    starting = (jnp.zeros((NX, NY, NZ), jnp.float32), jnp.zeros((NX, NY), jnp.float32))
    final_pair, leftover = lax.scan(deposit, starting, (flat_tiles, start_x, start_y))
    return final_pair


def reference(tiles, tile_block, tile_x, tile_y, psf, initial):
    observed_views = []
    norm_field = jnp.zeros((NX, NY, NZ), jnp.float32)
    for view_index in range(VIEWS):
        summed, counted = assemble(tiles[view_index], tile_block[view_index, :, :, 0], tile_x[view_index], tile_y[view_index])
        observed_views.append(summed / jnp.maximum(counted, 1.0)[:, :, None])
        coverage = jnp.broadcast_to(jnp.minimum(counted, 1.0)[:, :, None], (NX, NY, NZ))
        norm_field = norm_field + back_project(coverage, psf[view_index])
    estimate = initial
    for sweep_index in range(ITERS):
        correction = jnp.zeros((NX, NY, NZ), jnp.float32)
        for view_index in range(VIEWS):
            quotient = observed_views[view_index] / (blur(estimate, psf[view_index]) + soft_floor)
            correction = correction + back_project(quotient, psf[view_index])
        estimate = estimate * (correction + damping) / (norm_field + damping)
    return estimate
```

```python
import functools

import jax
import jax.numpy as jnp
from jax import lax
from jax.experimental import pallas as pl
from jax.experimental.pallas import tpu as pltpu
from jax.sharding import PartitionSpec as P

ITERS = 2
HALO_Y = 8

soft_floor = 0.01
damping = 0.5


def split_high_low(matrix):
    high = lax.reduce_precision(matrix, 8, 7)
    return high.astype(jnp.bfloat16), (matrix - high).astype(jnp.bfloat16)


def banded(taps, difference):
    summed = None
    for tap_index in range(taps.shape[-1]):
        term = jnp.where(difference == tap_index, taps[..., tap_index, None, None], 0.0)
        summed = term if summed is None else summed + term
    return summed


def place_kernel(filled, corner_x, corner_y, tiles, observed, summed, counted):
    view = pl.program_id(0)
    sources, _, capacity, wide, tall, _ = tiles.shape
    block_y = observed.shape[2]
    summed[...] = jnp.zeros_like(summed)
    counted[...] = jnp.zeros_like(counted)
    for source in range(sources):

        @pl.loop(0, capacity)
        def _(slot):
            at = source * capacity + slot

            @pl.when(filled[view, at] > 0)
            def _():
                x = corner_x[view, at]
                y = corner_y[view, at]
                where = (pl.ds(x, wide), pl.ds(y, tall), slice(None))
                summed[where] = summed[where] + tiles[source, 0, slot].astype(jnp.float32)
                counted[where] = counted[where] + 1.0

    @pl.loop(0, observed.shape[1])
    def _(x):
        observed[0, x] = summed[x, :block_y, :] / jnp.maximum(counted[x, :block_y, :], 1.0)


def place(filled, corner_x, corner_y, arrived, block_x, block_y):
    sources, views, capacity, wide, tall, depth = arrived.shape
    return pl.pallas_call(
        place_kernel,
        out_shape=jax.ShapeDtypeStruct((views, block_x, block_y, depth), jnp.float32),
        grid_spec=pltpu.PrefetchScalarGridSpec(
            num_scalar_prefetch=3,
            grid=(views,),
            in_specs=[
                pl.BlockSpec(
                    (sources, 1, capacity, wide, tall, depth), lambda v, *_: (0, v, 0, 0, 0, 0)
                )
            ],
            out_specs=pl.BlockSpec((1, block_x, block_y, depth), lambda v, *_: (v, 0, 0, 0)),
            scratch_shapes=[
                pltpu.VMEM((block_x, block_y, depth), jnp.float32),
                pltpu.VMEM((block_x, block_y, depth), jnp.float32),
            ],
        ),
        compiler_params=pltpu.CompilerParams(vmem_limit_bytes=32 << 20),
    )(filled, corner_x, corner_y, arrived)


def sweep_kernel(
    sizes,
    taps_x,
    observed,
    initial,
    inverse_norm,
    along_y,
    back_y,
    along_z,
    back_z,
    estimate,
    est_center,
    est_low,
    est_high,
    send_low,
    send_high,
    passed_y,
    passed_z,
    acc_center,
    out_x,
    out_y,
    in_x,
    in_y,
    vert_out,
    vert_in,
    est_send,
    est_recv,
    acc_send,
    acc_recv,
    vert_send,
    vert_recv,
):
    count_x, count_y = sizes
    views, block_x, block_y, depth = observed.shape
    tap_count = taps_x.shape[1]
    radius = tap_count // 2
    extended_x = block_x + 2 * radius
    me_x = lax.axis_index("gx")
    me_y = lax.axis_index("gy")
    me_v = lax.axis_index("vert")
    bf16 = jnp.bfloat16
    f32 = jnp.float32

    directions = [
        (dx, dy)
        for dx in (-1, 0, 1)
        for dy in (-1, 0, 1)
        if (dx, dy) != (0, 0)
    ]

    def exists(dx, dy):
        good = None
        for step, me, count in ((dx, me_x, count_x), (dy, me_y, count_y)):
            if step == -1:
                test = me > 0
            elif step == 1:
                test = me < count - 1
            else:
                continue
            good = test if good is None else jnp.logical_and(good, test)
        return good

    def device(dx, dy):
        return {"gx": me_x + dx, "gy": me_y + dy}

    def span(step):
        if step == 0:
            return pl.ds(radius, block_x)
        if step == -1:
            return pl.ds(radius, radius)
        return pl.ds(block_x, radius)

    def ghost(step):
        if step == 0:
            return pl.ds(radius, block_x)
        if step == -1:
            return pl.ds(0, radius)
        return pl.ds(block_x + radius, radius)

    def part(step, offset):
        if step == 0:
            return pl.ds(0, block_x)
        if step == -1:
            return pl.ds(0, radius)
        return pl.ds(block_x - radius, radius)

    def est_copy(sweep, index, dx, dy):
        if dy == 0:
            src = est_center.at[sweep, span(dx)]
            dst = est_center.at[sweep, ghost(-dx)]
        elif dy == -1:
            src = send_low.at[sweep, part(dx, 0)]
            dst = est_high.at[sweep, ghost(-dx)]
        else:
            src = send_high.at[sweep, part(dx, 0)]
            dst = est_low.at[sweep, ghost(-dx)]
        return src, dst

    def acc_copy(sweep, index, dx, dy):
        if dy == 0:
            side = 0 if dx == -1 else 1
            return out_x.at[sweep, side], in_x.at[sweep, 1 - side]
        side = 0 if dy == -1 else 1
        return out_y.at[sweep, side, ghost(dx)], in_y.at[sweep, 1 - side, ghost(-dx)]

    def exchange(make, send_sem, recv_sem, sweep):
        def copy(index, dx, dy):
            src, dst = make(sweep, index, dx, dy)
            opposite = directions.index((-dx, -dy))
            return pltpu.make_async_remote_copy(
                src_ref=src,
                dst_ref=dst,
                send_sem=send_sem.at[sweep, index],
                recv_sem=recv_sem.at[sweep, opposite],
                device_id=device(dx, dy),
                device_id_type=pl.DeviceIdType.MESH,
            )

        def start():
            for index, (dx, dy) in enumerate(directions):

                @pl.when(exists(dx, dy))
                def _():
                    copy(index, dx, dy).start()

        def finish():
            for index, (dx, dy) in enumerate(directions):

                @pl.when(exists(dx, dy))
                def _():
                    copy(index, dx, dy).wait_send()
                    opposite = directions.index((-dx, -dy))
                    src, dst = make(sweep, opposite, -dx, -dy)
                    pltpu.make_async_remote_copy(
                        src_ref=src,
                        dst_ref=dst,
                        send_sem=send_sem.at[sweep, opposite],
                        recv_sem=recv_sem.at[sweep, index],
                        device_id=device(dx, dy),
                        device_id_type=pl.DeviceIdType.MESH,
                    ).wait_recv()

        return start, finish

    barrier = pltpu.get_barrier_semaphore()
    for dx, dy in directions:

        @pl.when(exists(dx, dy))
        def _():
            pl.semaphore_signal(
                barrier, inc=1, device_id=device(dx, dy), device_id_type=pl.DeviceIdType.MESH
            )

    pl.semaphore_signal(
        barrier, inc=1, device_id={"vert": 1 - me_v}, device_id_type=pl.DeviceIdType.MESH
    )

    def publish(sweep, x, plane):
        est_center[sweep, radius + x] = plane.astype(bf16)
        send_low[sweep, x] = plane[:HALO_Y].astype(bf16)
        send_high[sweep, x] = plane[block_y - HALO_Y :].astype(bf16)

    @pl.loop(0, block_x)
    def _(x):
        publish(0, x, initial[x])

    for sweep in range(ITERS):
        for step in (-1, 1):

            @pl.when(jnp.logical_not(exists(step, 0)))
            def _():
                planes = ghost(step)
                est_center[sweep, planes] = jnp.zeros((radius, block_y, depth), bf16)
                est_low[sweep, planes] = jnp.zeros((radius, HALO_Y, depth), bf16)
                est_high[sweep, planes] = jnp.zeros((radius, HALO_Y, depth), bf16)
                in_x[sweep, 0 if step == -1 else 1] = jnp.zeros((radius, block_y, depth), bf16)
                in_y[sweep, 0, planes] = jnp.zeros((radius, HALO_Y, depth), bf16)
                in_y[sweep, 1, planes] = jnp.zeros((radius, HALO_Y, depth), bf16)

            @pl.when(jnp.logical_not(exists(0, step)))
            def _():
                rows = est_low if step == -1 else est_high
                rows[sweep] = jnp.zeros((extended_x, HALO_Y, depth), bf16)
                in_y[sweep, 0 if step == -1 else 1] = jnp.zeros((extended_x, HALO_Y, depth), bf16)

    passed_z[:, : 2 * radius] = jnp.zeros((views, 2 * radius, block_y, depth), f32)
    passed_z[:, 2 * radius + block_x :] = jnp.zeros((views, 2 * radius, block_y, depth), f32)

    peers = 1
    for dx, dy in directions:
        peers = peers + exists(dx, dy).astype(jnp.int32)
    pl.semaphore_wait(barrier, peers)

    group = 4
    while block_x % group:
        group //= 2

    for sweep in range(ITERS):
        start, finish = exchange(est_copy, est_send, est_recv, sweep)
        start()
        finish()

        @pl.loop(0, extended_x // 2)
        def _(pair):
            columns = []
            for x in (2 * pair, 2 * pair + 1):
                edges = jnp.concatenate(
                    [est_low[sweep, x].astype(f32), est_high[sweep, x].astype(f32)], axis=0
                ).astype(bf16)
                columns.append(jnp.concatenate([est_center[sweep, x], edges], axis=0))
            both = jnp.concatenate(columns, axis=1)
            both = jnp.concatenate([both, both], axis=0)
            result = jnp.dot(along_y[...], both, preferred_element_type=f32)
            for view in range(views):
                rows = slice(view * block_y, (view + 1) * block_y)
                passed_y[view, 2 * pair] = result[rows, :depth]
                passed_y[view, 2 * pair + 1] = result[rows, depth:]

        for view in range(views):

            @pl.loop(0, block_x // group)
            def _(step):
                planes = []
                for inner in range(group):
                    x = step * group + inner
                    value = taps_x[view, 0] * passed_y[view, x]
                    for tap in range(1, tap_count):
                        value = value + taps_x[view, tap] * passed_y[view, x + tap]
                    planes.append(value.astype(bf16))
                stacked = jnp.concatenate(planes, axis=0)
                stacked = jnp.concatenate([stacked, stacked], axis=1)
                blurred = jnp.dot(stacked, along_z[view], preferred_element_type=f32)
                measured = observed[view, pl.ds(step * group, group)].reshape(
                    group * block_y, depth
                )
                quotient = (measured / (blurred + soft_floor)).astype(bf16)
                quotient = jnp.concatenate([quotient, quotient], axis=1)
                spread = jnp.dot(quotient, back_z[view], preferred_element_type=f32)
                passed_z[view, pl.ds(2 * radius + step * group, group)] = spread.reshape(
                    group, block_y, depth
                )

        @pl.loop(0, extended_x // 2)
        def _(pair):
            columns = []
            for x in (2 * pair, 2 * pair + 1):
                stack = []
                for view in range(views):
                    value = taps_x[view, 0] * passed_z[view, x + 2 * radius]
                    for tap in range(1, tap_count):
                        value = value + taps_x[view, tap] * passed_z[view, x + 2 * radius - tap]
                    stack.append(value.astype(bf16))
                columns.append(jnp.concatenate(stack, axis=0))
            both = jnp.concatenate(columns, axis=1)
            result = jnp.dot(back_y[...], both, preferred_element_type=f32)
            rows = block_y + 2 * HALO_Y
            result = result[:rows] + result[rows:]
            for side in range(2):
                x = 2 * pair + side
                lanes = slice(side * depth, (side + 1) * depth)
                acc_center[x] = result[:block_y, lanes]
                out_y[sweep, 0, x] = result[block_y : block_y + HALO_Y, lanes].astype(bf16)
                out_y[sweep, 1, x] = result[block_y + HALO_Y :, lanes].astype(bf16)

        @pl.loop(0, radius)
        def _(x):
            out_x[sweep, 0, x] = acc_center[x].astype(bf16)
            out_x[sweep, 1, x] = acc_center[radius + block_x + x].astype(bf16)

        start, finish = exchange(acc_copy, acc_send, acc_recv, sweep)
        start()
        finish()

        @pl.loop(0, radius)
        def _(x):
            low = radius + x
            high = block_x + x
            acc_center[low] = acc_center[low] + in_x[sweep, 0, x].astype(f32)
            acc_center[high] = acc_center[high] + in_x[sweep, 1, x].astype(f32)
            for side in range(2):
                rows = slice(0, HALO_Y) if side == 0 else slice(block_y - HALO_Y, block_y)
                acc_center[low, rows] = acc_center[low, rows] + in_y[sweep, side, x].astype(f32)
                acc_center[high, rows] = acc_center[high, rows] + in_y[
                    sweep, side, radius + block_x + x
                ].astype(f32)

        @pl.loop(0, block_x)
        def _(x):
            plane = acc_center[radius + x]
            low = plane[:HALO_Y] + in_y[sweep, 0, radius + x].astype(f32)
            high = plane[block_y - HALO_Y :] + in_y[sweep, 1, radius + x].astype(f32)
            vert_out[sweep, x] = jnp.concatenate(
                [low, plane[HALO_Y : block_y - HALO_Y], high], axis=0
            )

        vert = pltpu.make_async_remote_copy(
            src_ref=vert_out.at[sweep],
            dst_ref=vert_in.at[sweep],
            send_sem=vert_send.at[sweep],
            recv_sem=vert_recv.at[sweep],
            device_id={"vert": 1 - me_v},
            device_id_type=pl.DeviceIdType.MESH,
        )
        vert.start()
        vert.wait()

        @pl.loop(0, block_x)
        def _(x):
            before = initial[x] if sweep == 0 else estimate[x]
            combined = vert_out[sweep, x] + vert_in[sweep, x]
            after = before * (combined + damping) * inverse_norm[x]
            estimate[x] = after
            if sweep + 1 < ITERS:
                publish(sweep + 1, x, after)


def sweeps(sizes, taps_x, observed, initial, inverse_norm, along_y, back_y, along_z, back_z):
    views, block_x, block_y, depth = observed.shape
    radius = taps_x.shape[1] // 2
    extended_x = block_x + 2 * radius
    vmem = pl.BlockSpec(memory_space=pltpu.VMEM)
    bf16 = jnp.bfloat16
    f32 = jnp.float32
    return pl.pallas_call(
        functools.partial(sweep_kernel, sizes),
        out_shape=jax.ShapeDtypeStruct(initial.shape, f32),
        in_specs=[pl.BlockSpec(memory_space=pltpu.SMEM)] + [vmem] * 7,
        out_specs=vmem,
        scratch_shapes=[
            pltpu.VMEM((ITERS, extended_x, block_y, depth), bf16),
            pltpu.VMEM((ITERS, extended_x, HALO_Y, depth), bf16),
            pltpu.VMEM((ITERS, extended_x, HALO_Y, depth), bf16),
            pltpu.VMEM((ITERS, block_x, HALO_Y, depth), bf16),
            pltpu.VMEM((ITERS, block_x, HALO_Y, depth), bf16),
            pltpu.VMEM((views, extended_x, block_y, depth), f32),
            pltpu.VMEM((views, block_x + 4 * radius, block_y, depth), f32),
            pltpu.VMEM((extended_x, block_y, depth), f32),
            pltpu.VMEM((ITERS, 2, radius, block_y, depth), bf16),
            pltpu.VMEM((ITERS, 2, extended_x, HALO_Y, depth), bf16),
            pltpu.VMEM((ITERS, 2, radius, block_y, depth), bf16),
            pltpu.VMEM((ITERS, 2, extended_x, HALO_Y, depth), bf16),
            pltpu.VMEM((ITERS, block_x, block_y, depth), f32),
            pltpu.VMEM((ITERS, block_x, block_y, depth), f32),
            pltpu.SemaphoreType.DMA((ITERS, 8)),
            pltpu.SemaphoreType.DMA((ITERS, 8)),
            pltpu.SemaphoreType.DMA((ITERS, 8)),
            pltpu.SemaphoreType.DMA((ITERS, 8)),
            pltpu.SemaphoreType.DMA((ITERS,)),
            pltpu.SemaphoreType.DMA((ITERS,)),
        ],
        compiler_params=pltpu.CompilerParams(
            collective_id=0, has_side_effects=True, vmem_limit_bytes=48 << 20
        ),
    )(taps_x, observed, initial, inverse_norm, along_y, back_y, along_z, back_z)


def shards(tiles, tile_block, tile_x, tile_y, psf, initial):
    column_count = lax.axis_size("gx")
    column_index = lax.axis_index("gx")
    row_index = lax.axis_index("gy")
    core_index = lax.axis_index("vert")
    local_views = tiles.shape[0]
    all_views = psf.shape[0]
    per_device = tiles.shape[2]
    tile_wide = tiles.shape[3]
    tile_tall = tiles.shape[4]
    block_x, block_y, depth = initial.shape
    capacity = max(2, 2 * per_device // column_count)
    radius = psf.shape[2] // 2
    first_view = core_index * local_views
    mine_psf = lax.dynamic_slice_in_dim(psf, first_view, local_views, 0)

    def my_rows(table):
        chosen = lax.dynamic_slice_in_dim(table, first_view, local_views, 0)
        chosen = lax.dynamic_slice_in_dim(chosen, row_index, 1, 1)[:, 0]
        return chosen.reshape(local_views, column_count, per_device)

    targets = my_rows(tile_block[:, :, :, 0])
    offsets_x = my_rows(tile_x)
    offsets_y = my_rows(tile_y)
    columns_iota = jnp.arange(column_count, dtype=jnp.int32)
    hits = (targets[..., None] == columns_iota).astype(jnp.int32)
    ranks = jnp.cumsum(hits, axis=2, dtype=jnp.int32)
    slot_ids = jnp.arange(capacity, dtype=jnp.int32) + 1
    sent_hits = jnp.swapaxes(lax.dynamic_slice_in_dim(hits, column_index, 1, 1)[:, 0], 1, 2)
    sent_ranks = jnp.swapaxes(lax.dynamic_slice_in_dim(ranks, column_index, 1, 1)[:, 0], 1, 2)
    chooser = sent_hits[:, :, None, :] * (
        sent_ranks[:, :, None, :] == slot_ids[None, None, :, None]
    ).astype(jnp.int32)
    outgoing = jnp.einsum(
        "vgkj,vjabz->gvkabz",
        chooser.astype(jnp.bfloat16),
        tiles[:, 0],
        preferred_element_type=jnp.bfloat16,
    )
    arrived = lax.all_to_all(outgoing, "gx", split_axis=0, concat_axis=0, tiled=True)
    from_hits = lax.dynamic_slice_in_dim(hits, column_index, 1, 3)[..., 0]
    from_ranks = lax.dynamic_slice_in_dim(ranks, column_index, 1, 3)[..., 0]
    picks = from_hits[:, :, None, :] * (
        from_ranks[:, :, None, :] == slot_ids[None, None, :, None]
    ).astype(jnp.int32)
    filled = jnp.sum(picks, axis=3).reshape(local_views, -1)
    corner_x = jnp.sum(picks * offsets_x[:, :, None, :], axis=3).reshape(local_views, -1)
    corner_y = jnp.sum(picks * offsets_y[:, :, None, :], axis=3).reshape(local_views, -1)
    observed = place(filled, corner_x, corner_y, arrived, block_x, block_y)

    row_iota = jnp.arange(tile_block.shape[1], dtype=jnp.int32)
    global_x = (tile_block[..., 0] * block_x + tile_x).reshape(all_views, -1)
    global_y = (row_iota[None, :, None] * block_y + tile_y).reshape(all_views, -1)
    near_x = jnp.arange(block_x + 2 * radius, dtype=jnp.int32) - radius
    near_y = jnp.arange(block_y + 2 * radius, dtype=jnp.int32) - radius
    cells_x = column_index * block_x + near_x
    cells_y = row_index * block_y + near_y
    cover_x = (
        (cells_x >= global_x[..., None]) & (cells_x < global_x[..., None] + tile_wide)
    ).astype(jnp.bfloat16)
    cover_y = (
        (cells_y >= global_y[..., None]) & (cells_y < global_y[..., None] + tile_tall)
    ).astype(jnp.bfloat16)
    counts = jnp.einsum("vti,vtj->vij", cover_x, cover_y, preferred_element_type=jnp.float32)
    coverage = jnp.minimum(counts, 1.0)
    iota_x = jnp.arange(block_x, dtype=jnp.int32)
    iota_y = jnp.arange(block_y, dtype=jnp.int32)
    iota_z = jnp.arange(depth, dtype=jnp.int32)
    adjoint_x = banded(psf[:, 0], iota_x[:, None] - near_x[None, :] + radius)
    adjoint_y = banded(psf[:, 1], iota_y[:, None] - near_y[None, :] + radius)
    exact = lax.Precision.HIGHEST
    spread = jnp.einsum("vij,vyj->viy", coverage, adjoint_y, precision=exact)
    spread = jnp.einsum("vxi,viy->vxy", adjoint_x, spread, precision=exact)
    profile = jnp.sum(banded(psf[:, 2], iota_z[:, None] - iota_z[None, :] + radius), axis=2)
    norm_field = jnp.einsum("vxy,vz->xyz", spread, profile, precision=exact)
    inverse_norm = 1.0 / (norm_field + damping)

    places_y = jnp.concatenate(
        [
            iota_y,
            jnp.arange(HALO_Y, dtype=jnp.int32) - HALO_Y,
            jnp.arange(HALO_Y, dtype=jnp.int32) + block_y,
        ]
    )
    band_y = banded(mine_psf[:, 1], places_y[None, :] - iota_y[:, None] + radius)
    high, low = split_high_low(band_y)
    flat = (local_views * block_y, places_y.shape[0])
    along_y = jnp.concatenate([high.reshape(flat), low.reshape(flat)], axis=1)
    back_y = jnp.concatenate([high.reshape(flat).T, low.reshape(flat).T], axis=0)
    band_z = banded(mine_psf[:, 2], iota_z[:, None] - iota_z[None, :] + radius)
    along_z = jnp.concatenate(split_high_low(band_z), axis=1)
    back_z = jnp.concatenate(split_high_low(jnp.swapaxes(band_z, 1, 2)), axis=1)
    return sweeps(
        (column_count, lax.axis_size("gy")),
        mine_psf[:, 0],
        observed,
        initial,
        inverse_norm,
        along_y,
        back_y,
        along_z,
        back_z,
    )


def solution(mesh):
    in_specs = (
        P("vert", "gy", ("groups", "gx"), None, None, None),
        P(None, None, "groups", None),
        P(None, None, "groups"),
        P(None, None, "groups"),
        P(),
        P(("groups", "gx"), "gy", None),
    )
    out_specs = P(("groups", "gx"), "gy", None)
    return jax.shard_map(shards, mesh=mesh, in_specs=in_specs, out_specs=out_specs, check_vma=False)
```

```python
import functools

import jax
import jax.numpy as jnp
from jax import lax
from jax.experimental import pallas as pl
from jax.experimental.pallas import tpu as pltpu
from jax.sharding import PartitionSpec as P

ITERS = 2
HALO_Y = 8

soft_floor = 0.01
damping = 0.5


def split_high_low(matrix):
    high = lax.reduce_precision(matrix, 8, 7)
    return high.astype(jnp.bfloat16), (matrix - high).astype(jnp.bfloat16)


def banded(taps, difference):
    summed = None
    for tap_index in range(taps.shape[-1]):
        term = jnp.where(difference == tap_index, taps[..., tap_index, None, None], 0.0)
        summed = term if summed is None else summed + term
    return summed


class Links:
    def __init__(self, sizes, radius, block_x):
        self.radius = radius
        self.block_x = block_x
        self.me = (lax.axis_index("gx"), lax.axis_index("gy"))
        self.sizes = sizes
        self.directions = [
            (dx, dy) for dx in (-1, 0, 1) for dy in (-1, 0, 1) if (dx, dy) != (0, 0)
        ]

    def exists(self, dx, dy):
        good = None
        for step, me, count in zip((dx, dy), self.me, self.sizes):
            if step == 0:
                continue
            test = me > 0 if step == -1 else me < count - 1
            good = test if good is None else jnp.logical_and(good, test)
        return good

    def device(self, dx, dy):
        return {"gx": self.me[0] + dx, "gy": self.me[1] + dy}

    def greet(self, others=()):
        barrier = pltpu.get_barrier_semaphore()
        for dx, dy in self.directions:

            @pl.when(self.exists(dx, dy))
            def _():
                pl.semaphore_signal(
                    barrier,
                    inc=1,
                    device_id=self.device(dx, dy),
                    device_id_type=pl.DeviceIdType.MESH,
                )

        for other in others:
            pl.semaphore_signal(
                barrier, inc=1, device_id=other, device_id_type=pl.DeviceIdType.MESH
            )

    def await_greetings(self, others=0):
        peers = others
        for dx, dy in self.directions:
            peers = peers + self.exists(dx, dy).astype(jnp.int32)
        pl.semaphore_wait(pltpu.get_barrier_semaphore(), peers)

    def span(self, step):
        if step == 0:
            return pl.ds(self.radius, self.block_x)
        return pl.ds(self.radius if step == -1 else self.block_x, self.radius)

    def ghost(self, step):
        if step == 0:
            return pl.ds(self.radius, self.block_x)
        return pl.ds(0 if step == -1 else self.block_x + self.radius, self.radius)

    def part(self, step):
        if step == 0:
            return pl.ds(0, self.block_x)
        return pl.ds(0 if step == -1 else self.block_x - self.radius, self.radius)

    def exchange(self, make, send_sem, recv_sem):
        def copy(index, dx, dy):
            src, dst = make(dx, dy)
            return pltpu.make_async_remote_copy(
                src_ref=src,
                dst_ref=dst,
                send_sem=send_sem.at[index],
                recv_sem=recv_sem.at[index],
                device_id=self.device(dx, dy),
                device_id_type=pl.DeviceIdType.MESH,
            )

        for index, (dx, dy) in enumerate(self.directions):

            @pl.when(self.exists(dx, dy))
            def _():
                copy(index, dx, dy).start()

        for index, (dx, dy) in enumerate(self.directions):

            @pl.when(self.exists(dx, dy))
            def _():
                copy(index, dx, dy).wait_send()

            @pl.when(self.exists(-dx, -dy))
            def _():
                copy(index, dx, dy).wait_recv()


def ghosts_of_estimate(links, center, low, high, send_low, send_high):
    def make(dx, dy):
        if dy == 0:
            return center.at[links.span(dx)], center.at[links.ghost(-dx)]
        if dy == -1:
            return send_low.at[links.part(dx)], high.at[links.ghost(-dx)]
        return send_high.at[links.part(dx)], low.at[links.ghost(-dx)]

    return make


def ghosts_of_sums(links, out_x, out_y, in_x, in_y):
    def make(dx, dy):
        if dy == 0:
            side = 0 if dx == -1 else 1
            return out_x.at[side], in_x.at[1 - side]
        side = 0 if dy == -1 else 1
        return out_y.at[side, links.ghost(dx)], in_y.at[1 - side, links.ghost(-dx)]

    return make


def clear_missing(links, center, low, high):
    radius = links.radius
    for step in (-1, 1):

        @pl.when(jnp.logical_not(links.exists(step, 0)))
        def _():
            for rows in (center, low, high):
                rows[links.ghost(step)] = jnp.zeros((radius,) + rows.shape[1:], rows.dtype)

        @pl.when(jnp.logical_not(links.exists(0, step)))
        def _():
            rows = low if step == -1 else high
            rows[...] = jnp.zeros(rows.shape, rows.dtype)

    tail = links.block_x + 2 * radius
    for rows in (center, low, high):
        rows[tail:] = jnp.zeros((rows.shape[0] - tail,) + rows.shape[1:], rows.dtype)


def publish(links, center, send_low, send_high, x, plane):
    center[links.radius + x] = plane.astype(jnp.bfloat16)
    send_low[x] = plane[:HALO_Y].astype(jnp.bfloat16)
    send_high[x] = plane[plane.shape[0] - HALO_Y :].astype(jnp.bfloat16)


def pass_along_y(center, low, high, along_y, passed_y, views):
    block_y, depth = center.shape[1:]

    @pl.loop(0, center.shape[0] // 4)
    def _(step):
        for first in (4 * step, 4 * step + 2):
            columns = []
            for x in (first, first + 1):
                edges = jnp.concatenate(
                    [low[x].astype(jnp.float32), high[x].astype(jnp.float32)], axis=0
                ).astype(jnp.bfloat16)
                columns.append(jnp.concatenate([center[x], edges], axis=0))
            both = jnp.concatenate(columns, axis=1)
            both = jnp.concatenate([both, both], axis=0)
            result = jnp.dot(along_y[...], both, preferred_element_type=jnp.float32)
            for view in range(views):
                rows = slice(view * block_y, (view + 1) * block_y)
                passed_y[view, first] = result[rows, :depth]
                passed_y[view, first + 1] = result[rows, depth:]


def pass_along_xz(taps_x, passed_y, along_z, view, first, group):
    planes = []
    for inner in range(group):
        x = first + inner
        value = taps_x[view, 0] * passed_y[view, x]
        for tap in range(1, taps_x.shape[1]):
            value = value + taps_x[view, tap] * passed_y[view, x + tap]
        planes.append(value.astype(jnp.bfloat16))
    stacked = jnp.concatenate(planes, axis=0)
    stacked = jnp.concatenate([stacked, stacked], axis=1)
    return jnp.dot(stacked, along_z, preferred_element_type=jnp.float32)


def spread_quotient(measured, blurred, back_z):
    quotient = (measured / (blurred + soft_floor)).astype(jnp.bfloat16)
    quotient = jnp.concatenate([quotient, quotient], axis=1)
    return jnp.dot(quotient, back_z, preferred_element_type=jnp.float32)


def group_of(block_x):
    group = 4
    while block_x % group:
        group //= 2
    return group


def blur_kernel(
    sizes,
    taps_x,
    initial,
    along_y,
    along_z,
    blurred,
    center,
    low,
    high,
    send_low,
    send_high,
    passed_y,
    send_sem,
    recv_sem,
):
    views, block_x, block_y, depth = blurred.shape
    links = Links(sizes, taps_x.shape[1] // 2, block_x)
    links.greet()

    @pl.loop(0, block_x)
    def _(x):
        publish(links, center, send_low, send_high, x, initial[x])

    clear_missing(links, center, low, high)
    links.await_greetings()
    links.exchange(
        ghosts_of_estimate(links, center, low, high, send_low, send_high), send_sem, recv_sem
    )
    pass_along_y(center, low, high, along_y, passed_y, views)
    group = group_of(block_x)

    @pl.loop(0, block_x // group)
    def _(step):
        for view in range(views):
            value = pass_along_xz(taps_x, passed_y, along_z[view], view, step * group, group)
            blurred[view, pl.ds(step * group, group)] = value.reshape(group, block_y, depth)


def estimate_scratch(planes, block_x, block_y, depth):
    return [
        pltpu.VMEM((planes, block_y, depth), jnp.bfloat16),
        pltpu.VMEM((planes, HALO_Y, depth), jnp.bfloat16),
        pltpu.VMEM((planes, HALO_Y, depth), jnp.bfloat16),
        pltpu.VMEM((block_x, HALO_Y, depth), jnp.bfloat16),
        pltpu.VMEM((block_x, HALO_Y, depth), jnp.bfloat16),
    ]


def planes_of(block_x, radius):
    return -(-(block_x + 2 * radius) // 4) * 4


def first_blur(sizes, taps_x, initial, along_y, along_z):
    block_x, block_y, depth = initial.shape
    views = taps_x.shape[0]
    planes = planes_of(block_x, taps_x.shape[1] // 2)
    vmem = pl.BlockSpec(memory_space=pltpu.VMEM)
    shape = (views, block_x, block_y, depth)
    return pl.pallas_call(
        functools.partial(blur_kernel, sizes),
        out_shape=jax.ShapeDtypeStruct(shape, jnp.float32),
        in_specs=[pl.BlockSpec(memory_space=pltpu.SMEM)] + [vmem] * 3,
        out_specs=vmem,
        scratch_shapes=estimate_scratch(planes, block_x, block_y, depth)
        + [
            pltpu.VMEM((views, planes, block_y, depth), jnp.float32),
            pltpu.SemaphoreType.DMA((8,)),
            pltpu.SemaphoreType.DMA((8,)),
        ],
        cost_estimate=pl.CostEstimate(
            flops=20_000_000_000, bytes_accessed=40_000_000, transcendentals=0
        ),
        compiler_params=pltpu.CompilerParams(
            collective_id=0, has_side_effects=True, vmem_limit_bytes=32 << 20
        ),
    )(taps_x, initial, along_y, along_z)


def place_kernel(
    filled, corner_x, corner_y, tiles, blurred, back_z, observed, spread, summed, counted
):
    sources, capacity, wide, tall, depth = tiles.shape
    block_x, block_y = observed.shape[:2]
    summed[...] = jnp.zeros_like(summed)
    counted[...] = jnp.zeros_like(counted)

    @pl.loop(0, sources)
    def _(source):
        @pl.loop(0, capacity)
        def _(slot):
            at = source * capacity + slot

            @pl.when(filled[at] > 0)
            def _():
                x = corner_x[at]
                y = corner_y[at]
                where = (pl.ds(x, wide), pl.ds(y, tall), slice(None))
                summed[where] = summed[where] + tiles[source, slot].astype(jnp.float32)
                counted[where] = counted[where] + 1.0

    group = group_of(block_x)

    @pl.loop(0, block_x // group)
    def _(step):
        planes = pl.ds(step * group, group)
        measured = summed[planes] / jnp.maximum(counted[planes], 1.0)
        observed[planes] = measured
        flat = (group * block_y, depth)
        result = spread_quotient(
            measured.reshape(flat), blurred[0, planes].reshape(flat), back_z[0]
        )
        spread[planes] = result.reshape(group, block_y, depth)


def place(view, filled, corner_x, corner_y, arrived, blurred, back_z):
    _, block_x, block_y, depth = blurred.shape
    shape = (block_x, block_y, depth)

    def whole(shape):
        return pl.BlockSpec(shape, lambda i, *_: (0,) * len(shape))

    return pl.pallas_call(
        place_kernel,
        out_shape=[jax.ShapeDtypeStruct(shape, jnp.float32)] * 2,
        grid_spec=pltpu.PrefetchScalarGridSpec(
            num_scalar_prefetch=3,
            grid=(1,),
            in_specs=[
                whole(arrived.shape),
                pl.BlockSpec((1,) + shape, lambda i, *_: (view, 0, 0, 0)),
                pl.BlockSpec((1,) + back_z.shape[1:], lambda i, *_: (view, 0, 0)),
            ],
            out_specs=[whole(shape)] * 2,
            scratch_shapes=[pltpu.VMEM(shape, jnp.float32)] * 2,
        ),
        cost_estimate=pl.CostEstimate(
            flops=1_000_000_000, bytes_accessed=8_000_000, transcendentals=0
        ),
        compiler_params=pltpu.CompilerParams(vmem_limit_bytes=24 << 20),
    )(filled, corner_x, corner_y, arrived, blurred, back_z)


def sweep_kernel(sizes, views, *refs):
    taps_x = refs[0]
    observed = refs[1 : 1 + views]
    spreads = refs[1 + views : 1 + 2 * views]
    initial, inverse_norm, along_y, back_y, along_z, back_z, estimate = refs[
        1 + 2 * views : 8 + 2 * views
    ]
    (
        center,
        low,
        high,
        send_low,
        send_high,
        passed_y,
        passed_z,
        acc,
        out_x,
        out_y,
        in_x,
        in_y,
        vert_out,
        vert_in,
        est_send,
        est_recv,
        acc_send,
        acc_recv,
        vert_send,
        vert_recv,
    ) = refs[8 + 2 * views :]
    block_x, block_y, depth = initial.shape
    tap_count = taps_x.shape[1]
    radius = tap_count // 2
    planes = center.shape[1]
    bf16 = jnp.bfloat16
    f32 = jnp.float32
    links = Links(sizes, radius, block_x)
    partner = {"vert": 1 - lax.axis_index("vert")}
    links.greet((partner,))
    for sweep in range(ITERS):
        if sweep > 0:
            at = sweep - 1
            clear_missing(links, center.at[at], low.at[at], high.at[at])
        for step in (-1, 1):
            side = 0 if step == -1 else 1

            @pl.when(jnp.logical_not(links.exists(step, 0)))
            def _():
                in_x[sweep, side] = jnp.zeros(in_x.shape[2:], bf16)
                for other in range(2):
                    in_y[sweep, other, links.ghost(step)] = jnp.zeros(
                        (radius,) + in_y.shape[3:], bf16
                    )

            @pl.when(jnp.logical_not(links.exists(0, step)))
            def _():
                in_y[sweep, side] = jnp.zeros(in_y.shape[2:], bf16)

    below = 2 * radius
    beyond = passed_z.shape[1] - below - block_x
    passed_z[:, :below] = jnp.zeros((views, below, block_y, depth), f32)
    passed_z[:, below + block_x :] = jnp.zeros((views, beyond, block_y, depth), f32)
    group = group_of(block_x)

    @pl.loop(0, block_x)
    def _(x):
        for view in range(views):
            passed_z[view, below + x] = spreads[view][x]

    for sweep in range(ITERS):
        if sweep > 0:
            at = sweep - 1
            links.exchange(
                ghosts_of_estimate(
                    links, center.at[at], low.at[at], high.at[at], send_low.at[at], send_high.at[at]
                ),
                est_send.at[at],
                est_recv.at[at],
            )
            pass_along_y(center.at[at], low.at[at], high.at[at], along_y, passed_y, views)

            @pl.loop(0, block_x // group)
            def _(step):
                first = step * group
                for view in range(views):
                    blurred = pass_along_xz(taps_x, passed_y, along_z[view], view, first, group)
                    measured = observed[view][pl.ds(first, group)].reshape(blurred.shape)
                    result = spread_quotient(measured, blurred, back_z[view])
                    passed_z[view, pl.ds(below + first, group)] = result.reshape(
                        group, block_y, depth
                    )

        @pl.loop(0, planes // 4)
        def _(step):
            for first in (4 * step, 4 * step + 2):
                columns = []
                for x in (first, first + 1):
                    stack = []
                    for view in range(views):
                        value = taps_x[view, 0] * passed_z[view, x + below]
                        for tap in range(1, tap_count):
                            value = value + taps_x[view, tap] * passed_z[view, x + below - tap]
                        stack.append(value.astype(bf16))
                    columns.append(jnp.concatenate(stack, axis=0))
                both = jnp.concatenate(columns, axis=1)
                result = jnp.dot(back_y[...], both, preferred_element_type=f32)
                rows = block_y + 2 * HALO_Y
                result = result[:rows] + result[rows:]
                for side in range(2):
                    x = first + side
                    lanes = slice(side * depth, (side + 1) * depth)
                    acc[x] = result[:block_y, lanes]
                    out_y[sweep, 0, x] = result[block_y : block_y + HALO_Y, lanes].astype(bf16)
                    out_y[sweep, 1, x] = result[block_y + HALO_Y :, lanes].astype(bf16)

        @pl.loop(0, radius)
        def _(x):
            out_x[sweep, 0, x] = acc[x].astype(bf16)
            out_x[sweep, 1, x] = acc[radius + block_x + x].astype(bf16)

        if sweep == 0:
            links.await_greetings(1)
        links.exchange(
            ghosts_of_sums(
                links, out_x.at[sweep], out_y.at[sweep], in_x.at[sweep], in_y.at[sweep]
            ),
            acc_send.at[sweep],
            acc_recv.at[sweep],
        )

        @pl.loop(0, radius)
        def _(x):
            for side, at, beside in ((0, radius + x, x), (1, block_x + x, radius + block_x + x)):
                plane = acc[at] + in_x[sweep, side, x].astype(f32)
                first = plane[:HALO_Y] + in_y[sweep, 0, beside].astype(f32)
                last = plane[block_y - HALO_Y :] + in_y[sweep, 1, beside].astype(f32)
                acc[at] = jnp.concatenate(
                    [first, plane[HALO_Y : block_y - HALO_Y], last], axis=0
                )

        @pl.loop(0, block_x)
        def _(x):
            plane = acc[radius + x]
            first = plane[:HALO_Y] + in_y[sweep, 0, radius + x].astype(f32)
            last = plane[block_y - HALO_Y :] + in_y[sweep, 1, radius + x].astype(f32)
            vert_out[sweep, x] = jnp.concatenate(
                [first, plane[HALO_Y : block_y - HALO_Y], last], axis=0
            )

        vert = pltpu.make_async_remote_copy(
            src_ref=vert_out.at[sweep],
            dst_ref=vert_in.at[sweep],
            send_sem=vert_send.at[sweep],
            recv_sem=vert_recv.at[sweep],
            device_id=partner,
            device_id_type=pl.DeviceIdType.MESH,
        )
        vert.start()
        vert.wait()

        @pl.loop(0, block_x)
        def _(x):
            before = initial[x] if sweep == 0 else estimate[x]
            combined = vert_out[sweep, x] + vert_in[sweep, x]
            after = before * (combined + damping) * inverse_norm[x]
            estimate[x] = after
            if sweep + 1 < ITERS:
                publish(
                    links, center.at[sweep], send_low.at[sweep], send_high.at[sweep], x, after
                )


def sweeps(
    sizes, taps_x, observed, spreads, initial, inverse_norm, along_y, back_y, along_z, back_z
):
    block_x, block_y, depth = initial.shape
    views = len(observed)
    radius = taps_x.shape[1] // 2
    planes = planes_of(block_x, radius)
    vmem = pl.BlockSpec(memory_space=pltpu.VMEM)
    bf16 = jnp.bfloat16
    f32 = jnp.float32
    repeats = ITERS - 1
    return pl.pallas_call(
        functools.partial(sweep_kernel, sizes, views),
        out_shape=jax.ShapeDtypeStruct(initial.shape, f32),
        in_specs=[pl.BlockSpec(memory_space=pltpu.SMEM)] + [vmem] * (6 + 2 * views),
        out_specs=vmem,
        scratch_shapes=[
            pltpu.VMEM((repeats,) + scratch.shape, scratch.dtype)
            for scratch in estimate_scratch(planes, block_x, block_y, depth)
        ]
        + [
            pltpu.VMEM((views, planes, block_y, depth), f32),
            pltpu.VMEM((views, planes + 2 * radius, block_y, depth), f32),
            pltpu.VMEM((planes, block_y, depth), f32),
            pltpu.VMEM((ITERS, 2, radius, block_y, depth), bf16),
            pltpu.VMEM((ITERS, 2, planes, HALO_Y, depth), bf16),
            pltpu.VMEM((ITERS, 2, radius, block_y, depth), bf16),
            pltpu.VMEM((ITERS, 2, planes, HALO_Y, depth), bf16),
            pltpu.VMEM((ITERS, block_x, block_y, depth), f32),
            pltpu.VMEM((ITERS, block_x, block_y, depth), f32),
            pltpu.SemaphoreType.DMA((repeats, 8)),
            pltpu.SemaphoreType.DMA((repeats, 8)),
            pltpu.SemaphoreType.DMA((ITERS, 8)),
            pltpu.SemaphoreType.DMA((ITERS, 8)),
            pltpu.SemaphoreType.DMA((ITERS,)),
            pltpu.SemaphoreType.DMA((ITERS,)),
        ],
        compiler_params=pltpu.CompilerParams(
            collective_id=1, has_side_effects=True, vmem_limit_bytes=52 << 20
        ),
    )(taps_x, *observed, *spreads, initial, inverse_norm, along_y, back_y, along_z, back_z)


def shards(tiles, tile_block, tile_x, tile_y, psf, initial):
    column_count = lax.axis_size("gx")
    column_index = lax.axis_index("gx")
    row_index = lax.axis_index("gy")
    core_index = lax.axis_index("vert")
    local_views = tiles.shape[0]
    all_views = psf.shape[0]
    per_device = tiles.shape[2]
    tile_wide = tiles.shape[3]
    tile_tall = tiles.shape[4]
    block_x, block_y, depth = initial.shape
    capacity = max(2, 2 * per_device // column_count)
    radius = psf.shape[2] // 2
    first_view = core_index * local_views
    mine_psf = lax.dynamic_slice_in_dim(psf, first_view, local_views, 0)

    def my_rows(table):
        chosen = lax.dynamic_slice_in_dim(table, first_view, local_views, 0)
        chosen = lax.dynamic_slice_in_dim(chosen, row_index, 1, 1)[:, 0]
        return chosen.reshape(local_views, column_count, per_device)

    targets = my_rows(tile_block[:, :, :, 0])
    offsets_x = my_rows(tile_x)
    offsets_y = my_rows(tile_y)
    columns_iota = jnp.arange(column_count, dtype=jnp.int32)
    hits = (targets[..., None] == columns_iota).astype(jnp.int32)
    ranks = jnp.cumsum(hits, axis=2, dtype=jnp.int32)
    slot_ids = jnp.arange(capacity, dtype=jnp.int32) + 1
    sent_hits = jnp.swapaxes(lax.dynamic_slice_in_dim(hits, column_index, 1, 1)[:, 0], 1, 2)
    sent_ranks = jnp.swapaxes(lax.dynamic_slice_in_dim(ranks, column_index, 1, 1)[:, 0], 1, 2)
    chooser = sent_hits[:, :, None, :] * (
        sent_ranks[:, :, None, :] == slot_ids[None, None, :, None]
    ).astype(jnp.int32)
    chooser = chooser.astype(jnp.bfloat16)
    arrived = []
    for view in range(local_views):
        outgoing = jnp.einsum(
            "gkj,jabz->gkabz",
            chooser[view],
            tiles[view, 0],
            preferred_element_type=jnp.bfloat16,
        )
        arrived.append(lax.all_to_all(outgoing, "gx", split_axis=0, concat_axis=0, tiled=True))
    from_hits = lax.dynamic_slice_in_dim(hits, column_index, 1, 3)[..., 0]
    from_ranks = lax.dynamic_slice_in_dim(ranks, column_index, 1, 3)[..., 0]
    picks = from_hits[:, :, None, :] * (
        from_ranks[:, :, None, :] == slot_ids[None, None, :, None]
    ).astype(jnp.int32)
    filled = jnp.sum(picks, axis=3).reshape(local_views, -1)
    corner_x = jnp.sum(picks * offsets_x[:, :, None, :], axis=3).reshape(local_views, -1)
    corner_y = jnp.sum(picks * offsets_y[:, :, None, :], axis=3).reshape(local_views, -1)

    row_iota = jnp.arange(tile_block.shape[1], dtype=jnp.int32)
    global_x = (tile_block[..., 0] * block_x + tile_x).reshape(all_views, -1)
    global_y = (row_iota[None, :, None] * block_y + tile_y).reshape(all_views, -1)
    near_x = jnp.arange(block_x + 2 * radius, dtype=jnp.int32) - radius
    near_y = jnp.arange(block_y + 2 * radius, dtype=jnp.int32) - radius
    cells_x = column_index * block_x + near_x
    cells_y = row_index * block_y + near_y
    cover_x = (
        (cells_x >= global_x[..., None]) & (cells_x < global_x[..., None] + tile_wide)
    ).astype(jnp.bfloat16)
    cover_y = (
        (cells_y >= global_y[..., None]) & (cells_y < global_y[..., None] + tile_tall)
    ).astype(jnp.bfloat16)
    counts = jnp.einsum("vti,vtj->vij", cover_x, cover_y, preferred_element_type=jnp.float32)
    coverage = jnp.minimum(counts, 1.0)
    iota_x = jnp.arange(block_x, dtype=jnp.int32)
    iota_y = jnp.arange(block_y, dtype=jnp.int32)
    iota_z = jnp.arange(depth, dtype=jnp.int32)
    adjoint_x = banded(psf[:, 0], iota_x[:, None] - near_x[None, :] + radius)
    adjoint_y = banded(psf[:, 1], iota_y[:, None] - near_y[None, :] + radius)
    exact = lax.Precision.HIGHEST
    spread = jnp.einsum("vij,vyj->viy", coverage, adjoint_y, precision=exact)
    spread = jnp.einsum("vxi,viy->vxy", adjoint_x, spread, precision=exact)
    profile = jnp.sum(banded(psf[:, 2], iota_z[:, None] - iota_z[None, :] + radius), axis=2)
    norm_field = jnp.einsum("vxy,vz->xyz", spread, profile, precision=exact)
    inverse_norm = 1.0 / (norm_field + damping)

    places_y = jnp.concatenate(
        [
            iota_y,
            jnp.arange(HALO_Y, dtype=jnp.int32) - HALO_Y,
            jnp.arange(HALO_Y, dtype=jnp.int32) + block_y,
        ]
    )
    band_y = banded(mine_psf[:, 1], places_y[None, :] - iota_y[:, None] + radius)
    high, low = split_high_low(band_y)
    flat = (local_views * block_y, places_y.shape[0])
    along_y = jnp.concatenate([high.reshape(flat), low.reshape(flat)], axis=1)
    back_y = jnp.concatenate([high.reshape(flat).T, low.reshape(flat).T], axis=0)
    band_z = banded(mine_psf[:, 2], iota_z[:, None] - iota_z[None, :] + radius)
    along_z = jnp.concatenate(split_high_low(band_z), axis=1)
    back_z = jnp.concatenate(split_high_low(jnp.swapaxes(band_z, 1, 2)), axis=1)
    sizes = (column_count, lax.axis_size("gy"))
    taps_x = mine_psf[:, 0]
    blurred = first_blur(sizes, taps_x, initial, along_y, along_z)
    placed = [
        place(
            view, filled[view], corner_x[view], corner_y[view], arrived[view], blurred, back_z
        )
        for view in range(local_views)
    ]
    observed, spreads = zip(*placed)
    return sweeps(
        sizes,
        taps_x,
        observed,
        spreads,
        initial,
        inverse_norm,
        along_y,
        back_y,
        along_z,
        back_z,
    )


def solution(mesh):
    in_specs = (
        P("vert", "gy", ("groups", "gx"), None, None, None),
        P(None, None, "groups", None),
        P(None, None, "groups"),
        P(None, None, "groups"),
        P(),
        P(("groups", "gx"), "gy", None),
    )
    out_specs = P(("groups", "gx"), "gy", None)
    return jax.shard_map(shards, mesh=mesh, in_specs=in_specs, out_specs=out_specs, check_vma=False)
```

```python
import functools

import jax
import jax.numpy as jnp
from jax import lax
from jax.experimental import pallas as pl
from jax.experimental.pallas import tpu as pltpu
from jax.sharding import PartitionSpec as P

ITERS = 2
HALO_Y = 8

soft_floor = 0.01
damping = 0.5


def split_high_low(matrix):
    high = lax.reduce_precision(matrix, 8, 7)
    return high.astype(jnp.bfloat16), (matrix - high).astype(jnp.bfloat16)


def banded(taps, difference):
    summed = None
    for tap_index in range(taps.shape[-1]):
        term = jnp.where(difference == tap_index, taps[..., tap_index, None, None], 0.0)
        summed = term if summed is None else summed + term
    return summed


class Links:
    def __init__(self, sizes, radius, block_x):
        self.radius = radius
        self.block_x = block_x
        self.me = (lax.axis_index("gx"), lax.axis_index("gy"))
        self.sizes = sizes
        self.directions = [
            (dx, dy) for dx in (-1, 0, 1) for dy in (-1, 0, 1) if (dx, dy) != (0, 0)
        ]

    def exists(self, dx, dy):
        good = None
        for step, me, count in zip((dx, dy), self.me, self.sizes):
            if step == 0:
                continue
            test = me > 0 if step == -1 else me < count - 1
            good = test if good is None else jnp.logical_and(good, test)
        return good

    def device(self, dx, dy):
        return {"gx": self.me[0] + dx, "gy": self.me[1] + dy}

    def greet(self, others=()):
        barrier = pltpu.get_barrier_semaphore()
        for dx, dy in self.directions:

            @pl.when(self.exists(dx, dy))
            def _():
                pl.semaphore_signal(
                    barrier,
                    inc=1,
                    device_id=self.device(dx, dy),
                    device_id_type=pl.DeviceIdType.MESH,
                )

        for other in others:
            pl.semaphore_signal(
                barrier, inc=1, device_id=other, device_id_type=pl.DeviceIdType.MESH
            )

    def await_greetings(self, others=0):
        peers = others
        for dx, dy in self.directions:
            peers = peers + self.exists(dx, dy).astype(jnp.int32)
        pl.semaphore_wait(pltpu.get_barrier_semaphore(), peers)

    def span(self, step):
        if step == 0:
            return pl.ds(self.radius, self.block_x)
        return pl.ds(self.radius if step == -1 else self.block_x, self.radius)

    def ghost(self, step):
        if step == 0:
            return pl.ds(self.radius, self.block_x)
        return pl.ds(0 if step == -1 else self.block_x + self.radius, self.radius)

    def part(self, step):
        if step == 0:
            return pl.ds(0, self.block_x)
        return pl.ds(0 if step == -1 else self.block_x - self.radius, self.radius)

    def exchange(self, make, send_sem, recv_sem):
        def copy(index, dx, dy):
            src, dst = make(dx, dy)
            return pltpu.make_async_remote_copy(
                src_ref=src,
                dst_ref=dst,
                send_sem=send_sem.at[index],
                recv_sem=recv_sem.at[index],
                device_id=self.device(dx, dy),
                device_id_type=pl.DeviceIdType.MESH,
            )

        for index, (dx, dy) in enumerate(self.directions):

            @pl.when(self.exists(dx, dy))
            def _():
                copy(index, dx, dy).start()

        for index, (dx, dy) in enumerate(self.directions):

            @pl.when(self.exists(dx, dy))
            def _():
                copy(index, dx, dy).wait_send()

            @pl.when(self.exists(-dx, -dy))
            def _():
                copy(index, dx, dy).wait_recv()


def ghosts_of_estimate(links, center, low, high, send_low, send_high):
    def make(dx, dy):
        if dy == 0:
            return center.at[links.span(dx)], center.at[links.ghost(-dx)]
        if dy == -1:
            return send_low.at[links.part(dx)], high.at[links.ghost(-dx)]
        return send_high.at[links.part(dx)], low.at[links.ghost(-dx)]

    return make


def ghosts_of_sums(links, out_x, out_y, in_x, in_y):
    def make(dx, dy):
        if dy == 0:
            side = 0 if dx == -1 else 1
            return out_x.at[side], in_x.at[1 - side]
        side = 0 if dy == -1 else 1
        return out_y.at[side, links.ghost(dx)], in_y.at[1 - side, links.ghost(-dx)]

    return make


def clear_missing(links, center, low, high):
    radius = links.radius
    for step in (-1, 1):

        @pl.when(jnp.logical_not(links.exists(step, 0)))
        def _():
            for rows in (center, low, high):
                rows[links.ghost(step)] = jnp.zeros((radius,) + rows.shape[1:], rows.dtype)

        @pl.when(jnp.logical_not(links.exists(0, step)))
        def _():
            rows = low if step == -1 else high
            rows[...] = jnp.zeros(rows.shape, rows.dtype)

    tail = links.block_x + 2 * radius
    for rows in (center, low, high):
        rows[tail:] = jnp.zeros((rows.shape[0] - tail,) + rows.shape[1:], rows.dtype)


def publish(links, center, send_low, send_high, x, plane):
    center[links.radius + x] = plane.astype(jnp.bfloat16)
    send_low[x] = plane[:HALO_Y].astype(jnp.bfloat16)
    send_high[x] = plane[plane.shape[0] - HALO_Y :].astype(jnp.bfloat16)


def pass_along_y(center, low, high, along_y, passed_y, views):
    block_y, depth = center.shape[1:]

    @pl.loop(0, center.shape[0] // 4)
    def _(step):
        for first in (4 * step, 4 * step + 2):
            columns = []
            for x in (first, first + 1):
                edges = jnp.concatenate(
                    [low[x].astype(jnp.float32), high[x].astype(jnp.float32)], axis=0
                ).astype(jnp.bfloat16)
                columns.append(jnp.concatenate([center[x], edges], axis=0))
            both = jnp.concatenate(columns, axis=1)
            both = jnp.concatenate([both, both], axis=0)
            result = jnp.dot(along_y[...], both, preferred_element_type=jnp.float32)
            for view in range(views):
                rows = slice(view * block_y, (view + 1) * block_y)
                passed_y[view, first] = result[rows, :depth]
                passed_y[view, first + 1] = result[rows, depth:]


def pass_along_xz(taps_x, passed_y, along_z, view, first, group):
    planes = []
    for inner in range(group):
        x = first + inner
        value = taps_x[view, 0] * passed_y[view, x]
        for tap in range(1, taps_x.shape[1]):
            value = value + taps_x[view, tap] * passed_y[view, x + tap]
        planes.append(value.astype(jnp.bfloat16))
    stacked = jnp.concatenate(planes, axis=0)
    stacked = jnp.concatenate([stacked, stacked], axis=1)
    return jnp.dot(stacked, along_z, preferred_element_type=jnp.float32)


def spread_quotient(measured, blurred, back_z):
    quotient = (measured / (blurred + soft_floor)).astype(jnp.bfloat16)
    quotient = jnp.concatenate([quotient, quotient], axis=1)
    return jnp.dot(quotient, back_z, preferred_element_type=jnp.float32)


def group_of(block_x):
    group = 4
    while block_x % group:
        group //= 2
    return group


def halo_kernel(
    sizes, radius, initial, center, low, high, all_center, all_low, all_high, *scratch
):
    send_low, send_high, send_sem, recv_sem = scratch
    block_x = initial.shape[0]
    links = Links(sizes, radius, block_x)
    links.greet()

    @pl.loop(0, block_x)
    def _(x):
        publish(links, all_center, send_low, send_high, x, initial[x])

    clear_missing(links, all_center, all_low, all_high)
    links.await_greetings()
    links.exchange(
        ghosts_of_estimate(links, all_center, all_low, all_high, send_low, send_high),
        send_sem,
        recv_sem,
    )

    @pl.loop(0, center.shape[0])
    def _(x):
        center[x] = all_center[x]
        low[x] = all_low[x]
        high[x] = all_high[x]


def blur_kernel(taps_x, center, low, high, along_y, along_z, blurred, passed_y):
    views, block_x, block_y, depth = blurred.shape
    pass_along_y(center, low, high, along_y, passed_y, views)
    group = group_of(block_x)

    @pl.loop(0, block_x // group)
    def _(step):
        for view in range(views):
            value = pass_along_xz(taps_x, passed_y, along_z[view], view, step * group, group)
            blurred[view, pl.ds(step * group, group)] = value.reshape(group, block_y, depth)


def estimate_scratch(planes, block_x, block_y, depth):
    return [
        pltpu.VMEM((planes, block_y, depth), jnp.bfloat16),
        pltpu.VMEM((planes, HALO_Y, depth), jnp.bfloat16),
        pltpu.VMEM((planes, HALO_Y, depth), jnp.bfloat16),
        pltpu.VMEM((block_x, HALO_Y, depth), jnp.bfloat16),
        pltpu.VMEM((block_x, HALO_Y, depth), jnp.bfloat16),
    ]


def planes_of(block_x, radius):
    return -(-(block_x + 2 * radius) // 4) * 4


def first_halos(sizes, radius, initial):
    block_x, block_y, depth = initial.shape
    vmem = pl.BlockSpec(memory_space=pltpu.VMEM)
    scratch = estimate_scratch(planes_of(block_x, radius), block_x, block_y, depth)
    return pl.pallas_call(
        functools.partial(halo_kernel, sizes, radius),
        out_shape=[jax.ShapeDtypeStruct(one.shape, one.dtype) for one in scratch[:3]],
        in_specs=[vmem],
        out_specs=[vmem] * 3,
        scratch_shapes=scratch
        + [pltpu.SemaphoreType.DMA((8,)), pltpu.SemaphoreType.DMA((8,))],
        compiler_params=pltpu.CompilerParams(
            collective_id=0, has_side_effects=True, vmem_limit_bytes=12 << 20
        ),
    )(initial)


def first_blur(taps_x, halos, along_y, along_z, block_x):
    planes, block_y, depth = halos[0].shape
    views = taps_x.shape[0]
    vmem = pl.BlockSpec(memory_space=pltpu.VMEM)
    shape = (views, block_x, block_y, depth)
    return pl.pallas_call(
        blur_kernel,
        out_shape=jax.ShapeDtypeStruct(shape, jnp.float32),
        in_specs=[pl.BlockSpec(memory_space=pltpu.SMEM)] + [vmem] * 5,
        out_specs=vmem,
        scratch_shapes=[pltpu.VMEM((views, planes, block_y, depth), jnp.float32)],
        cost_estimate=pl.CostEstimate(
            flops=10_000_000_000, bytes_accessed=40_000_000, transcendentals=0
        ),
        compiler_params=pltpu.CompilerParams(vmem_limit_bytes=20 << 20),
    )(taps_x, *halos, along_y, along_z)


def place_kernel(
    filled, corner_x, corner_y, tiles, blurred, back_z, observed, spread, summed, counted
):
    view = pl.program_id(0)
    sources, _, capacity, wide, tall, depth = tiles.shape
    _, block_x, block_y, _ = observed.shape
    summed[...] = jnp.zeros_like(summed)
    counted[...] = jnp.zeros_like(counted)

    @pl.loop(0, sources)
    def _(source):
        @pl.loop(0, capacity)
        def _(slot):
            at = source * capacity + slot

            @pl.when(filled[view, at] > 0)
            def _():
                x = corner_x[view, at]
                y = corner_y[view, at]
                where = (pl.ds(x, wide), pl.ds(y, tall), slice(None))
                summed[where] = summed[where] + tiles[source, 0, slot].astype(jnp.float32)
                counted[where] = counted[where] + 1.0

    group = group_of(block_x)

    @pl.loop(0, block_x // group)
    def _(step):
        planes = pl.ds(step * group, group)
        measured = summed[planes] / jnp.maximum(counted[planes], 1.0)
        observed[0, planes] = measured
        flat = (group * block_y, depth)
        result = spread_quotient(
            measured.reshape(flat), blurred[0, planes].reshape(flat), back_z[0]
        )
        spread[0, planes] = result.reshape(group, block_y, depth)


def place(filled, corner_x, corner_y, arrived, blurred, back_z):
    sources, views, capacity, wide, tall, depth = arrived.shape
    shape = blurred.shape
    volume = pl.BlockSpec((1,) + shape[1:], lambda v, *_: (v, 0, 0, 0))
    return pl.pallas_call(
        place_kernel,
        out_shape=[jax.ShapeDtypeStruct(shape, jnp.float32)] * 2,
        grid_spec=pltpu.PrefetchScalarGridSpec(
            num_scalar_prefetch=3,
            grid=(views,),
            in_specs=[
                pl.BlockSpec(
                    (sources, 1, capacity, wide, tall, depth), lambda v, *_: (0, v, 0, 0, 0, 0)
                ),
                volume,
                pl.BlockSpec((1,) + back_z.shape[1:], lambda v, *_: (v, 0, 0)),
            ],
            out_specs=[volume] * 2,
            scratch_shapes=[pltpu.VMEM(shape[1:], jnp.float32)] * 2,
        ),
        compiler_params=pltpu.CompilerParams(vmem_limit_bytes=20 << 20),
    )(filled, corner_x, corner_y, arrived, blurred, back_z)


def sweep_kernel(sizes, *refs):
    (
        taps_x,
        observed,
        spreads,
        initial,
        inverse_norm,
        along_y,
        back_y,
        along_z,
        back_z,
        estimate,
        center,
        low,
        high,
        send_low,
        send_high,
        passed_y,
        passed_z,
        acc,
        out_x,
        out_y,
        in_x,
        in_y,
        far_x,
        far_y,
        vert_in,
        est_send,
        est_recv,
        acc_send,
        acc_recv,
        vert_send,
        vert_recv,
        far_send,
        far_recv,
    ) = refs
    views, block_x, block_y, depth = observed.shape
    tap_count = taps_x.shape[1]
    radius = tap_count // 2
    planes = center.shape[1]
    bf16 = jnp.bfloat16
    f32 = jnp.float32
    links = Links(sizes, radius, block_x)
    partner = {"vert": 1 - lax.axis_index("vert")}
    links.greet((partner,))
    for sweep in range(ITERS):
        if sweep > 0:
            at = sweep - 1
            clear_missing(links, center.at[at], low.at[at], high.at[at])
        for step in (-1, 1):
            side = 0 if step == -1 else 1

            @pl.when(jnp.logical_not(links.exists(step, 0)))
            def _():
                in_x[sweep, side] = jnp.zeros(in_x.shape[2:], bf16)
                for other in range(2):
                    in_y[sweep, other, links.ghost(step)] = jnp.zeros(
                        (radius,) + in_y.shape[3:], bf16
                    )

            @pl.when(jnp.logical_not(links.exists(0, step)))
            def _():
                in_y[sweep, side] = jnp.zeros(in_y.shape[2:], bf16)

    below = 2 * radius
    beyond = passed_z.shape[1] - below - block_x
    passed_z[:, :below] = jnp.zeros((views, below, block_y, depth), f32)
    passed_z[:, below + block_x :] = jnp.zeros((views, beyond, block_y, depth), f32)
    group = group_of(block_x)

    @pl.loop(0, block_x)
    def _(x):
        for view in range(views):
            passed_z[view, below + x] = spreads[view, x]

    for sweep in range(ITERS):
        if sweep > 0:
            at = sweep - 1
            links.exchange(
                ghosts_of_estimate(
                    links, center.at[at], low.at[at], high.at[at], send_low.at[at], send_high.at[at]
                ),
                est_send.at[at],
                est_recv.at[at],
            )
            pass_along_y(center.at[at], low.at[at], high.at[at], along_y, passed_y, views)

            @pl.loop(0, block_x // group)
            def _(step):
                first = step * group
                for view in range(views):
                    blurred = pass_along_xz(taps_x, passed_y, along_z[view], view, first, group)
                    measured = observed[view, pl.ds(first, group)].reshape(blurred.shape)
                    result = spread_quotient(measured, blurred, back_z[view])
                    passed_z[view, pl.ds(below + first, group)] = result.reshape(
                        group, block_y, depth
                    )

        if sweep == 0:
            links.await_greetings(1)

        def vert(start, size):
            chunk = pl.ds(start, size)
            return pltpu.make_async_remote_copy(
                src_ref=acc.at[sweep, chunk],
                dst_ref=vert_in.at[sweep, chunk],
                send_sem=vert_send.at[sweep],
                recv_sem=vert_recv.at[sweep],
                device_id=partner,
                device_id_type=pl.DeviceIdType.MESH,
            )

        first_chunk = radius // 4
        last_chunk = (radius + block_x - 1) // 4

        @pl.loop(0, planes // 4)
        def _(step):
            for first in (4 * step, 4 * step + 2):
                columns = []
                for x in (first, first + 1):
                    stack = []
                    for view in range(views):
                        value = taps_x[view, 0] * passed_z[view, x + below]
                        for tap in range(1, tap_count):
                            value = value + taps_x[view, tap] * passed_z[view, x + below - tap]
                        stack.append(value.astype(bf16))
                    columns.append(jnp.concatenate(stack, axis=0))
                both = jnp.concatenate(columns, axis=1)
                result = jnp.dot(back_y[...], both, preferred_element_type=f32)
                rows = block_y + 2 * HALO_Y
                result = result[:rows] + result[rows:]
                for side in range(2):
                    x = first + side
                    lanes = slice(side * depth, (side + 1) * depth)
                    acc[sweep, x] = result[:block_y, lanes]
                    out_y[sweep, 0, x] = result[block_y : block_y + HALO_Y, lanes].astype(bf16)
                    out_y[sweep, 1, x] = result[block_y + HALO_Y :, lanes].astype(bf16)

            @pl.when(jnp.logical_and(step >= first_chunk, step <= last_chunk))
            def _():
                vert(4 * step, 4).start()

        @pl.loop(0, radius)
        def _(x):
            out_x[sweep, 0, x] = acc[sweep, x].astype(bf16)
            out_x[sweep, 1, x] = acc[sweep, radius + block_x + x].astype(bf16)

        links.exchange(
            ghosts_of_sums(
                links, out_x.at[sweep], out_y.at[sweep], in_x.at[sweep], in_y.at[sweep]
            ),
            acc_send.at[sweep],
            acc_recv.at[sweep],
        )
        forwards = [
            pltpu.make_async_remote_copy(
                src_ref=near.at[sweep],
                dst_ref=far.at[sweep],
                send_sem=far_send.at[sweep, index],
                recv_sem=far_recv.at[sweep, index],
                device_id=partner,
                device_id_type=pl.DeviceIdType.MESH,
            )
            for index, (near, far) in enumerate(((in_x, far_x), (in_y, far_y)))
        ]
        for forward in forwards:
            forward.start()
        vert(4 * first_chunk, 4 * (last_chunk - first_chunk + 1)).wait()

        @pl.loop(0, block_x)
        def _(x):
            acc[sweep, radius + x] = acc[sweep, radius + x] + vert_in[sweep, radius + x]

        for forward in forwards:
            forward.wait()

        def beyond_y(side, plane):
            return in_y[sweep, side, plane].astype(f32) + far_y[sweep, side, plane].astype(f32)

        @pl.loop(0, radius)
        def _(x):
            for side, at, beside in ((0, radius + x, x), (1, block_x + x, radius + block_x + x)):
                plane = acc[sweep, at] + (
                    in_x[sweep, side, x].astype(f32) + far_x[sweep, side, x].astype(f32)
                )
                first = plane[:HALO_Y] + beyond_y(0, beside)
                last = plane[block_y - HALO_Y :] + beyond_y(1, beside)
                acc[sweep, at] = jnp.concatenate(
                    [first, plane[HALO_Y : block_y - HALO_Y], last], axis=0
                )

        @pl.loop(0, block_x)
        def _(x):
            plane = acc[sweep, radius + x]
            first = plane[:HALO_Y] + beyond_y(0, radius + x)
            last = plane[block_y - HALO_Y :] + beyond_y(1, radius + x)
            combined = jnp.concatenate([first, plane[HALO_Y : block_y - HALO_Y], last], axis=0)
            before = initial[x] if sweep == 0 else estimate[x]
            after = before * (combined + damping) * inverse_norm[x]
            estimate[x] = after
            if sweep + 1 < ITERS:
                publish(
                    links, center.at[sweep], send_low.at[sweep], send_high.at[sweep], x, after
                )


def sweeps(
    sizes, taps_x, observed, spreads, initial, inverse_norm, along_y, back_y, along_z, back_z
):
    block_x, block_y, depth = initial.shape
    views = observed.shape[0]
    radius = taps_x.shape[1] // 2
    planes = planes_of(block_x, radius)
    extended_x = block_x + 2 * radius
    vmem = pl.BlockSpec(memory_space=pltpu.VMEM)
    bf16 = jnp.bfloat16
    f32 = jnp.float32
    repeats = ITERS - 1
    return pl.pallas_call(
        functools.partial(sweep_kernel, sizes),
        out_shape=jax.ShapeDtypeStruct(initial.shape, f32),
        in_specs=[pl.BlockSpec(memory_space=pltpu.SMEM)] + [vmem] * 8,
        out_specs=vmem,
        scratch_shapes=[
            pltpu.VMEM((repeats,) + scratch.shape, scratch.dtype)
            for scratch in estimate_scratch(planes, block_x, block_y, depth)
        ]
        + [
            pltpu.VMEM((views, planes, block_y, depth), f32),
            pltpu.VMEM((views, planes + 2 * radius, block_y, depth), f32),
            pltpu.VMEM((ITERS, planes, block_y, depth), f32),
            pltpu.VMEM((ITERS, 2, radius, block_y, depth), bf16),
            pltpu.VMEM((ITERS, 2, planes, HALO_Y, depth), bf16),
            pltpu.VMEM((ITERS, 2, radius, block_y, depth), bf16),
            pltpu.VMEM((ITERS, 2, extended_x, HALO_Y, depth), bf16),
            pltpu.VMEM((ITERS, 2, radius, block_y, depth), bf16),
            pltpu.VMEM((ITERS, 2, extended_x, HALO_Y, depth), bf16),
            pltpu.VMEM((ITERS, planes, block_y, depth), f32),
            pltpu.SemaphoreType.DMA((repeats, 8)),
            pltpu.SemaphoreType.DMA((repeats, 8)),
            pltpu.SemaphoreType.DMA((ITERS, 8)),
            pltpu.SemaphoreType.DMA((ITERS, 8)),
            pltpu.SemaphoreType.DMA((ITERS,)),
            pltpu.SemaphoreType.DMA((ITERS,)),
            pltpu.SemaphoreType.DMA((ITERS, 2)),
            pltpu.SemaphoreType.DMA((ITERS, 2)),
        ],
        compiler_params=pltpu.CompilerParams(
            collective_id=1, has_side_effects=True, vmem_limit_bytes=40 << 20
        ),
    )(taps_x, observed, spreads, initial, inverse_norm, along_y, back_y, along_z, back_z)


def shards(tiles, tile_block, tile_x, tile_y, psf, initial):
    column_count = lax.axis_size("gx")
    column_index = lax.axis_index("gx")
    row_index = lax.axis_index("gy")
    core_index = lax.axis_index("vert")
    local_views = tiles.shape[0]
    all_views = psf.shape[0]
    per_device = tiles.shape[2]
    tile_wide = tiles.shape[3]
    tile_tall = tiles.shape[4]
    block_x, block_y, depth = initial.shape
    capacity = max(2, 2 * per_device // column_count)
    radius = psf.shape[2] // 2
    first_view = core_index * local_views
    mine_psf = lax.dynamic_slice_in_dim(psf, first_view, local_views, 0)

    def my_rows(table):
        chosen = lax.dynamic_slice_in_dim(table, first_view, local_views, 0)
        chosen = lax.dynamic_slice_in_dim(chosen, row_index, 1, 1)[:, 0]
        return chosen.reshape(local_views, column_count, per_device)

    targets = my_rows(tile_block[:, :, :, 0])
    offsets_x = my_rows(tile_x)
    offsets_y = my_rows(tile_y)
    columns_iota = jnp.arange(column_count, dtype=jnp.int32)
    hits = (targets[..., None] == columns_iota).astype(jnp.int32)
    ranks = jnp.cumsum(hits, axis=2, dtype=jnp.int32)
    slot_ids = jnp.arange(capacity, dtype=jnp.int32) + 1
    sent_hits = jnp.swapaxes(lax.dynamic_slice_in_dim(hits, column_index, 1, 1)[:, 0], 1, 2)
    sent_ranks = jnp.swapaxes(lax.dynamic_slice_in_dim(ranks, column_index, 1, 1)[:, 0], 1, 2)
    chooser = sent_hits[:, :, None, :] * (
        sent_ranks[:, :, None, :] == slot_ids[None, None, :, None]
    ).astype(jnp.int32)
    outgoing = jnp.einsum(
        "vgkj,vjabz->gvkabz",
        chooser.astype(jnp.bfloat16),
        tiles[:, 0],
        preferred_element_type=jnp.bfloat16,
    )
    sizes = (column_count, lax.axis_size("gy"))
    halos = first_halos(sizes, radius, initial)
    outgoing, halos = lax.optimization_barrier((outgoing, halos))
    arrived = lax.all_to_all(outgoing, "gx", split_axis=0, concat_axis=0, tiled=True)
    from_hits = lax.dynamic_slice_in_dim(hits, column_index, 1, 3)[..., 0]
    from_ranks = lax.dynamic_slice_in_dim(ranks, column_index, 1, 3)[..., 0]
    picks = from_hits[:, :, None, :] * (
        from_ranks[:, :, None, :] == slot_ids[None, None, :, None]
    ).astype(jnp.int32)
    filled = jnp.sum(picks, axis=3).reshape(local_views, -1)
    corner_x = jnp.sum(picks * offsets_x[:, :, None, :], axis=3).reshape(local_views, -1)
    corner_y = jnp.sum(picks * offsets_y[:, :, None, :], axis=3).reshape(local_views, -1)

    row_iota = jnp.arange(tile_block.shape[1], dtype=jnp.int32)
    global_x = (tile_block[..., 0] * block_x + tile_x).reshape(all_views, -1)
    global_y = (row_iota[None, :, None] * block_y + tile_y).reshape(all_views, -1)
    near_x = jnp.arange(block_x + 2 * radius, dtype=jnp.int32) - radius
    near_y = jnp.arange(block_y + 2 * radius, dtype=jnp.int32) - radius
    cells_x = column_index * block_x + near_x
    cells_y = row_index * block_y + near_y
    cover_x = (
        (cells_x >= global_x[..., None]) & (cells_x < global_x[..., None] + tile_wide)
    ).astype(jnp.bfloat16)
    cover_y = (
        (cells_y >= global_y[..., None]) & (cells_y < global_y[..., None] + tile_tall)
    ).astype(jnp.bfloat16)
    counts = jnp.einsum("vti,vtj->vij", cover_x, cover_y, preferred_element_type=jnp.float32)
    coverage = jnp.minimum(counts, 1.0)
    iota_x = jnp.arange(block_x, dtype=jnp.int32)
    iota_y = jnp.arange(block_y, dtype=jnp.int32)
    iota_z = jnp.arange(depth, dtype=jnp.int32)
    adjoint_x = banded(psf[:, 0], iota_x[:, None] - near_x[None, :] + radius)
    adjoint_y = banded(psf[:, 1], iota_y[:, None] - near_y[None, :] + radius)
    exact = lax.Precision.HIGHEST
    spread = jnp.einsum("vij,vyj->viy", coverage, adjoint_y, precision=exact)
    spread = jnp.einsum("vxi,viy->vxy", adjoint_x, spread, precision=exact)
    profile = jnp.sum(banded(psf[:, 2], iota_z[:, None] - iota_z[None, :] + radius), axis=2)
    norm_field = jnp.einsum("vxy,vz->xyz", spread, profile, precision=exact)
    inverse_norm = 1.0 / (norm_field + damping)

    places_y = jnp.concatenate(
        [
            iota_y,
            jnp.arange(HALO_Y, dtype=jnp.int32) - HALO_Y,
            jnp.arange(HALO_Y, dtype=jnp.int32) + block_y,
        ]
    )
    band_y = banded(mine_psf[:, 1], places_y[None, :] - iota_y[:, None] + radius)
    high, low = split_high_low(band_y)
    flat = (local_views * block_y, places_y.shape[0])
    along_y = jnp.concatenate([high.reshape(flat), low.reshape(flat)], axis=1)
    back_y = jnp.concatenate([high.reshape(flat).T, low.reshape(flat).T], axis=0)
    band_z = banded(mine_psf[:, 2], iota_z[:, None] - iota_z[None, :] + radius)
    along_z = jnp.concatenate(split_high_low(band_z), axis=1)
    back_z = jnp.concatenate(split_high_low(jnp.swapaxes(band_z, 1, 2)), axis=1)
    taps_x = mine_psf[:, 0]
    blurred = first_blur(taps_x, halos, along_y, along_z, block_x)
    observed, spreads = place(filled, corner_x, corner_y, arrived, blurred, back_z)
    return sweeps(
        sizes,
        taps_x,
        observed,
        spreads,
        initial,
        inverse_norm,
        along_y,
        back_y,
        along_z,
        back_z,
    )


def solution(mesh):
    in_specs = (
        P("vert", "gy", ("groups", "gx"), None, None, None),
        P(None, None, "groups", None),
        P(None, None, "groups"),
        P(None, None, "groups"),
        P(),
        P(("groups", "gx"), "gy", None),
    )
    out_specs = P(("groups", "gx"), "gy", None)
    return jax.shard_map(shards, mesh=mesh, in_specs=in_specs, out_specs=out_specs, check_vma=False)
```

```python
import functools

import jax
import jax.numpy as jnp
from jax import lax
from jax.experimental import pallas as pl
from jax.experimental.pallas import tpu as pltpu
from jax.sharding import PartitionSpec as P

ITERS = 2
HALO_Y = 8

soft_floor = 0.01
damping = 0.5


def split_high_low(matrix):
    high = lax.reduce_precision(matrix, 8, 7)
    return high.astype(jnp.bfloat16), (matrix - high).astype(jnp.bfloat16)


def banded(taps, difference):
    summed = None
    for tap_index in range(taps.shape[-1]):
        term = jnp.where(difference == tap_index, taps[..., tap_index, None, None], 0.0)
        summed = term if summed is None else summed + term
    return summed


class Links:
    def __init__(self, sizes, radius, block_x):
        self.radius = radius
        self.block_x = block_x
        self.me = (lax.axis_index("gx"), lax.axis_index("gy"))
        self.sizes = sizes
        self.directions = [
            (dx, dy) for dx in (-1, 0, 1) for dy in (-1, 0, 1) if (dx, dy) != (0, 0)
        ]

    def exists(self, dx, dy):
        good = None
        for step, me, count in zip((dx, dy), self.me, self.sizes):
            if step == 0:
                continue
            test = me > 0 if step == -1 else me < count - 1
            good = test if good is None else jnp.logical_and(good, test)
        return good

    def device(self, dx, dy):
        return {"gx": self.me[0] + dx, "gy": self.me[1] + dy}

    def greet(self, others=()):
        barrier = pltpu.get_barrier_semaphore()
        for dx, dy in self.directions:

            @pl.when(self.exists(dx, dy))
            def _():
                pl.semaphore_signal(
                    barrier,
                    inc=1,
                    device_id=self.device(dx, dy),
                    device_id_type=pl.DeviceIdType.MESH,
                )

        for other in others:
            pl.semaphore_signal(
                barrier, inc=1, device_id=other, device_id_type=pl.DeviceIdType.MESH
            )

    def await_greetings(self, others=0):
        peers = others
        for dx, dy in self.directions:
            peers = peers + self.exists(dx, dy).astype(jnp.int32)
        pl.semaphore_wait(pltpu.get_barrier_semaphore(), peers)

    def span(self, step):
        if step == 0:
            return pl.ds(self.radius, self.block_x)
        return pl.ds(self.radius if step == -1 else self.block_x, self.radius)

    def ghost(self, step):
        if step == 0:
            return pl.ds(self.radius, self.block_x)
        return pl.ds(0 if step == -1 else self.block_x + self.radius, self.radius)

    def part(self, step):
        if step == 0:
            return pl.ds(0, self.block_x)
        return pl.ds(0 if step == -1 else self.block_x - self.radius, self.radius)

    def exchange(self, make, send_sem, recv_sem):
        self.start(make, send_sem, recv_sem, self.directions)
        self.finish(make, send_sem, recv_sem, self.directions)

    def across_x(self):
        return [one for one in self.directions if one[0] != 0]

    def along_y_only(self):
        return [one for one in self.directions if one[0] == 0]

    def copy(self, make, send_sem, recv_sem, dx, dy):
        index = self.directions.index((dx, dy))
        src, dst = make(dx, dy)
        return pltpu.make_async_remote_copy(
            src_ref=src,
            dst_ref=dst,
            send_sem=send_sem.at[index],
            recv_sem=recv_sem.at[index],
            device_id=self.device(dx, dy),
            device_id_type=pl.DeviceIdType.MESH,
        )

    def start(self, make, send_sem, recv_sem, directions):
        for dx, dy in directions:

            @pl.when(self.exists(dx, dy))
            def _():
                self.copy(make, send_sem, recv_sem, dx, dy).start()

    def finish(self, make, send_sem, recv_sem, directions):
        for dx, dy in directions:

            @pl.when(self.exists(dx, dy))
            def _():
                self.copy(make, send_sem, recv_sem, dx, dy).wait_send()

            @pl.when(self.exists(-dx, -dy))
            def _():
                self.copy(make, send_sem, recv_sem, dx, dy).wait_recv()


def ghosts_of_estimate(links, center, low, high, send_low, send_high):
    def make(dx, dy):
        if dy == 0:
            return center.at[links.span(dx)], center.at[links.ghost(-dx)]
        if dy == -1:
            return send_low.at[links.part(dx)], high.at[links.ghost(-dx)]
        return send_high.at[links.part(dx)], low.at[links.ghost(-dx)]

    return make


def ghosts_of_sums(links, out_x, out_y, in_x, in_y):
    def make(dx, dy):
        if dy == 0:
            side = 0 if dx == -1 else 1
            return out_x.at[side], in_x.at[1 - side]
        side = 0 if dy == -1 else 1
        return out_y.at[side, links.ghost(dx)], in_y.at[1 - side, links.ghost(-dx)]

    return make


def clear_missing(links, center, low, high):
    radius = links.radius
    for step in (-1, 1):

        @pl.when(jnp.logical_not(links.exists(step, 0)))
        def _():
            for rows in (center, low, high):
                rows[links.ghost(step)] = jnp.zeros((radius,) + rows.shape[1:], rows.dtype)

        @pl.when(jnp.logical_not(links.exists(0, step)))
        def _():
            rows = low if step == -1 else high
            rows[...] = jnp.zeros(rows.shape, rows.dtype)

    tail = links.block_x + 2 * radius
    for rows in (center, low, high):
        rows[tail:] = jnp.zeros((rows.shape[0] - tail,) + rows.shape[1:], rows.dtype)


def publish(links, center, send_low, send_high, x, plane):
    center[links.radius + x] = plane.astype(jnp.bfloat16)
    send_low[x] = plane[:HALO_Y].astype(jnp.bfloat16)
    send_high[x] = plane[plane.shape[0] - HALO_Y :].astype(jnp.bfloat16)


def pass_along_y(center, low, high, along_y, passed_y, views):
    block_y, depth = center.shape[1:]

    @pl.loop(0, center.shape[0] // 4)
    def _(step):
        for first in (4 * step, 4 * step + 2):
            columns = []
            for x in (first, first + 1):
                edges = jnp.concatenate(
                    [low[x].astype(jnp.float32), high[x].astype(jnp.float32)], axis=0
                ).astype(jnp.bfloat16)
                columns.append(jnp.concatenate([center[x], edges], axis=0))
            both = jnp.concatenate(columns, axis=1)
            both = jnp.concatenate([both, both], axis=0)
            result = jnp.dot(along_y[...], both, preferred_element_type=jnp.float32)
            for view in range(views):
                rows = slice(view * block_y, (view + 1) * block_y)
                passed_y[view, first] = result[rows, :depth]
                passed_y[view, first + 1] = result[rows, depth:]


def pass_along_xz(taps_x, passed_y, along_z, view, first, group):
    planes = []
    for inner in range(group):
        x = first + inner
        value = taps_x[view, 0] * passed_y[view, x]
        for tap in range(1, taps_x.shape[1]):
            value = value + taps_x[view, tap] * passed_y[view, x + tap]
        planes.append(value.astype(jnp.bfloat16))
    stacked = jnp.concatenate(planes, axis=0)
    stacked = jnp.concatenate([stacked, stacked], axis=1)
    return jnp.dot(stacked, along_z, preferred_element_type=jnp.float32)


def spread_quotient(measured, blurred, back_z):
    quotient = (measured / (blurred + soft_floor)).astype(jnp.bfloat16)
    quotient = jnp.concatenate([quotient, quotient], axis=1)
    return jnp.dot(quotient, back_z, preferred_element_type=jnp.float32)


def group_of(block_x):
    group = 4
    while block_x % group:
        group //= 2
    return group


def halo_kernel(
    sizes, radius, initial, center, low, high, all_center, all_low, all_high, *scratch
):
    send_low, send_high, send_sem, recv_sem = scratch
    block_x = initial.shape[0]
    links = Links(sizes, radius, block_x)
    links.greet()

    @pl.loop(0, block_x)
    def _(x):
        publish(links, all_center, send_low, send_high, x, initial[x])

    clear_missing(links, all_center, all_low, all_high)
    links.await_greetings()
    links.exchange(
        ghosts_of_estimate(links, all_center, all_low, all_high, send_low, send_high),
        send_sem,
        recv_sem,
    )

    @pl.loop(0, center.shape[0])
    def _(x):
        center[x] = all_center[x]
        low[x] = all_low[x]
        high[x] = all_high[x]


def blur_kernel(taps_x, center, low, high, along_y, along_z, blurred, passed_y):
    views, block_x, block_y, depth = blurred.shape
    pass_along_y(center, low, high, along_y, passed_y, views)
    group = group_of(block_x)

    @pl.loop(0, block_x // group)
    def _(step):
        for view in range(views):
            value = pass_along_xz(taps_x, passed_y, along_z[view], view, step * group, group)
            blurred[view, pl.ds(step * group, group)] = value.reshape(group, block_y, depth)


def estimate_scratch(planes, block_x, block_y, depth):
    return [
        pltpu.VMEM((planes, block_y, depth), jnp.bfloat16),
        pltpu.VMEM((planes, HALO_Y, depth), jnp.bfloat16),
        pltpu.VMEM((planes, HALO_Y, depth), jnp.bfloat16),
        pltpu.VMEM((block_x, HALO_Y, depth), jnp.bfloat16),
        pltpu.VMEM((block_x, HALO_Y, depth), jnp.bfloat16),
    ]


def planes_of(block_x, radius):
    return -(-(block_x + 2 * radius) // 4) * 4


def first_halos(sizes, radius, initial):
    block_x, block_y, depth = initial.shape
    vmem = pl.BlockSpec(memory_space=pltpu.VMEM)
    scratch = estimate_scratch(planes_of(block_x, radius), block_x, block_y, depth)
    return pl.pallas_call(
        functools.partial(halo_kernel, sizes, radius),
        out_shape=[jax.ShapeDtypeStruct(one.shape, one.dtype) for one in scratch[:3]],
        in_specs=[vmem],
        out_specs=[vmem] * 3,
        scratch_shapes=scratch
        + [pltpu.SemaphoreType.DMA((8,)), pltpu.SemaphoreType.DMA((8,))],
        compiler_params=pltpu.CompilerParams(
            collective_id=0, has_side_effects=True, vmem_limit_bytes=12 << 20
        ),
    )(initial)


def first_blur(taps_x, halos, along_y, along_z, block_x):
    planes, block_y, depth = halos[0].shape
    views = taps_x.shape[0]
    vmem = pl.BlockSpec(memory_space=pltpu.VMEM)
    shape = (views, block_x, block_y, depth)
    return pl.pallas_call(
        blur_kernel,
        out_shape=jax.ShapeDtypeStruct(shape, jnp.float32),
        in_specs=[pl.BlockSpec(memory_space=pltpu.SMEM)] + [vmem] * 5,
        out_specs=vmem,
        scratch_shapes=[pltpu.VMEM((views, planes, block_y, depth), jnp.float32)],
        cost_estimate=pl.CostEstimate(
            flops=10_000_000_000, bytes_accessed=40_000_000, transcendentals=0
        ),
        compiler_params=pltpu.CompilerParams(vmem_limit_bytes=20 << 20),
    )(taps_x, *halos, along_y, along_z)


def place_kernel(
    below, filled, corner_x, corner_y, tiles, blurred, back_z, observed, spread, summed, counted
):
    view = pl.program_id(0)
    sources, _, capacity, wide, tall, depth = tiles.shape
    _, block_x, block_y, _ = observed.shape
    summed[...] = jnp.zeros_like(summed)
    counted[...] = jnp.zeros_like(counted)

    @pl.loop(0, sources)
    def _(source):
        @pl.loop(0, capacity)
        def _(slot):
            at = source * capacity + slot

            @pl.when(filled[view, at] > 0)
            def _():
                x = corner_x[view, at]
                y = corner_y[view, at]
                where = (pl.ds(x, wide), pl.ds(y, tall), slice(None))
                summed[where] = summed[where] + tiles[source, 0, slot].astype(jnp.float32)
                counted[where] = counted[where] + 1.0

    group = group_of(block_x)
    beyond = spread.shape[1] - below - block_x
    spread[0, :below] = jnp.zeros((below, block_y, depth), jnp.float32)
    spread[0, below + block_x :] = jnp.zeros((beyond, block_y, depth), jnp.float32)

    @pl.loop(0, block_x // group)
    def _(step):
        planes = pl.ds(step * group, group)
        measured = summed[planes] / jnp.maximum(counted[planes], 1.0)
        observed[0, planes] = measured
        flat = (group * block_y, depth)
        result = spread_quotient(
            measured.reshape(flat), blurred[0, planes].reshape(flat), back_z[0]
        )
        spread[0, pl.ds(below + step * group, group)] = result.reshape(group, block_y, depth)


def place(filled, corner_x, corner_y, arrived, blurred, back_z, radius):
    sources, views, capacity, wide, tall, depth = arrived.shape
    shape = blurred.shape
    volume = pl.BlockSpec((1,) + shape[1:], lambda v, *_: (v, 0, 0, 0))
    padded = (views, planes_of(shape[1], radius) + 2 * radius) + shape[2:]
    return pl.pallas_call(
        functools.partial(place_kernel, 2 * radius),
        out_shape=[
            jax.ShapeDtypeStruct(shape, jnp.float32),
            jax.ShapeDtypeStruct(padded, jnp.float32),
        ],
        grid_spec=pltpu.PrefetchScalarGridSpec(
            num_scalar_prefetch=3,
            grid=(views,),
            in_specs=[
                pl.BlockSpec(
                    (sources, 1, capacity, wide, tall, depth), lambda v, *_: (0, v, 0, 0, 0, 0)
                ),
                volume,
                pl.BlockSpec((1,) + back_z.shape[1:], lambda v, *_: (v, 0, 0)),
            ],
            out_specs=[
                volume,
                pl.BlockSpec((1,) + padded[1:], lambda v, *_: (v, 0, 0, 0)),
            ],
            scratch_shapes=[pltpu.VMEM(shape[1:], jnp.float32)] * 2,
        ),
        compiler_params=pltpu.CompilerParams(vmem_limit_bytes=20 << 20),
    )(filled, corner_x, corner_y, arrived, blurred, back_z)


def sweep_kernel(sizes, *refs):
    (
        taps_x,
        observed,
        spreads,
        initial,
        inverse_norm,
        along_y,
        back_y,
        along_z,
        back_z,
        estimate,
        center,
        low,
        high,
        send_low,
        send_high,
        passed_y,
        passed_z,
        acc,
        out_x,
        out_y,
        in_x,
        in_y,
        far_x,
        far_y,
        vert_in,
        est_send,
        est_recv,
        acc_send,
        acc_recv,
        vert_send,
        vert_recv,
        far_send,
        far_recv,
    ) = refs
    views, block_x, block_y, depth = observed.shape
    tap_count = taps_x.shape[1]
    radius = tap_count // 2
    planes = center.shape[1]
    bf16 = jnp.bfloat16
    f32 = jnp.float32
    links = Links(sizes, radius, block_x)
    partner = {"vert": 1 - lax.axis_index("vert")}
    links.greet((partner,))
    for sweep in range(ITERS):
        if sweep > 0:
            at = sweep - 1
            clear_missing(links, center.at[at], low.at[at], high.at[at])
        for step in (-1, 1):
            side = 0 if step == -1 else 1

            @pl.when(jnp.logical_not(links.exists(step, 0)))
            def _():
                in_x[sweep, side] = jnp.zeros(in_x.shape[2:], bf16)
                for other in range(2):
                    in_y[sweep, other, links.ghost(step)] = jnp.zeros(
                        (radius,) + in_y.shape[3:], bf16
                    )

            @pl.when(jnp.logical_not(links.exists(0, step)))
            def _():
                in_y[sweep, side] = jnp.zeros(in_y.shape[2:], bf16)

    below = 2 * radius
    beyond = passed_z.shape[1] - below - block_x
    passed_z[:, :below] = jnp.zeros((views, below, block_y, depth), f32)
    passed_z[:, below + block_x :] = jnp.zeros((views, beyond, block_y, depth), f32)
    group = group_of(block_x)

    for sweep in range(ITERS):
        if sweep > 0:
            at = sweep - 1
            pass_along_y(center.at[at], low.at[at], high.at[at], along_y, passed_y, views)

            @pl.loop(0, block_x // group)
            def _(step):
                first = step * group
                for view in range(views):
                    blurred = pass_along_xz(taps_x, passed_y, along_z[view], view, first, group)
                    measured = observed[view, pl.ds(first, group)].reshape(blurred.shape)
                    result = spread_quotient(measured, blurred, back_z[view])
                    passed_z[view, pl.ds(below + first, group)] = result.reshape(
                        group, block_y, depth
                    )

        if sweep == 0:
            links.await_greetings(1)

        def vert(start, size):
            chunk = pl.ds(start, size)
            return pltpu.make_async_remote_copy(
                src_ref=acc.at[sweep, chunk],
                dst_ref=vert_in.at[sweep, chunk],
                send_sem=vert_send.at[sweep],
                recv_sem=vert_recv.at[sweep],
                device_id=partner,
                device_id_type=pl.DeviceIdType.MESH,
            )

        first_chunk = radius // 4
        last_chunk = (radius + block_x - 1) // 4

        source = spreads if sweep == 0 else passed_z
        far_chunk = (radius + block_x) // 4
        edge_turns = planes // 4 - far_chunk + -(-radius // 4)
        def adjoint(turn):
            step = lax.rem(turn + far_chunk, planes // 4)
            for first in (4 * step, 4 * step + 2):
                columns = []
                for x in (first, first + 1):
                    stack = []
                    for view in range(views):
                        value = taps_x[view, 0] * source[view, x + below]
                        for tap in range(1, tap_count):
                            value = value + taps_x[view, tap] * source[view, x + below - tap]
                        stack.append(value.astype(bf16))
                    columns.append(jnp.concatenate(stack, axis=0))
                both = jnp.concatenate(columns, axis=1)
                result = jnp.dot(back_y[...], both, preferred_element_type=f32)
                rows = block_y + 2 * HALO_Y
                result = result[:rows] + result[rows:]
                for side in range(2):
                    x = first + side
                    lanes = slice(side * depth, (side + 1) * depth)
                    acc[sweep, x] = result[:block_y, lanes]
                    out_y[sweep, 0, x] = result[block_y : block_y + HALO_Y, lanes].astype(bf16)
                    out_y[sweep, 1, x] = result[block_y + HALO_Y :, lanes].astype(bf16)

            @pl.when(jnp.logical_and(step >= first_chunk, step <= last_chunk))
            def _():
                vert(4 * step, 4).start()

        sums = (
            ghosts_of_sums(
                links, out_x.at[sweep], out_y.at[sweep], in_x.at[sweep], in_y.at[sweep]
            ),
            acc_send.at[sweep],
            acc_recv.at[sweep],
        )

        @pl.loop(0, edge_turns)
        def _(turn):
            adjoint(turn)

        @pl.loop(0, radius)
        def _(x):
            out_x[sweep, 0, x] = acc[sweep, x].astype(bf16)
            out_x[sweep, 1, x] = acc[sweep, radius + block_x + x].astype(bf16)

        links.start(*sums, links.across_x())

        @pl.loop(edge_turns, planes // 4)
        def _(turn):
            adjoint(turn)

        links.start(*sums, links.along_y_only())
        links.finish(*sums, links.across_x())
        links.finish(*sums, links.along_y_only())
        forwards = [
            pltpu.make_async_remote_copy(
                src_ref=near.at[sweep],
                dst_ref=far.at[sweep],
                send_sem=far_send.at[sweep, index],
                recv_sem=far_recv.at[sweep, index],
                device_id=partner,
                device_id_type=pl.DeviceIdType.MESH,
            )
            for index, (near, far) in enumerate(((in_x, far_x), (in_y, far_y)))
        ]
        for forward in forwards:
            forward.start()
        vert(4 * first_chunk, 4 * (last_chunk - first_chunk + 1)).wait()

        @pl.loop(0, block_x)
        def _(x):
            acc[sweep, radius + x] = acc[sweep, radius + x] + vert_in[sweep, radius + x]

        for forward in forwards:
            forward.wait()

        def beyond_y(side, plane):
            return in_y[sweep, side, plane].astype(f32) + far_y[sweep, side, plane].astype(f32)

        @pl.loop(0, radius)
        def _(x):
            for side, at, beside in ((0, radius + x, x), (1, block_x + x, radius + block_x + x)):
                plane = acc[sweep, at] + (
                    in_x[sweep, side, x].astype(f32) + far_x[sweep, side, x].astype(f32)
                )
                first = plane[:HALO_Y] + beyond_y(0, beside)
                last = plane[block_y - HALO_Y :] + beyond_y(1, beside)
                acc[sweep, at] = jnp.concatenate(
                    [first, plane[HALO_Y : block_y - HALO_Y], last], axis=0
                )

        def update(x):
            plane = acc[sweep, radius + x]
            first = plane[:HALO_Y] + beyond_y(0, radius + x)
            last = plane[block_y - HALO_Y :] + beyond_y(1, radius + x)
            combined = jnp.concatenate([first, plane[HALO_Y : block_y - HALO_Y], last], axis=0)
            before = initial[x] if sweep == 0 else estimate[x]
            after = before * (combined + damping) * inverse_norm[x]
            estimate[x] = after
            if sweep + 1 < ITERS:
                publish(
                    links, center.at[sweep], send_low.at[sweep], send_high.at[sweep], x, after
                )

        if sweep + 1 < ITERS:
            news = (
                ghosts_of_estimate(
                    links,
                    center.at[sweep],
                    low.at[sweep],
                    high.at[sweep],
                    send_low.at[sweep],
                    send_high.at[sweep],
                ),
                est_send.at[sweep],
                est_recv.at[sweep],
            )

            @pl.loop(0, radius)
            def _(x):
                update(x)
                update(block_x - radius + x)

            links.start(*news, links.across_x())

            @pl.loop(radius, block_x - radius)
            def _(x):
                update(x)

            links.start(*news, links.along_y_only())
            links.finish(*news, links.directions)
        else:

            @pl.loop(0, block_x)
            def _(x):
                update(x)


def sweeps(
    sizes, taps_x, observed, spreads, initial, inverse_norm, along_y, back_y, along_z, back_z
):
    block_x, block_y, depth = initial.shape
    views = observed.shape[0]
    radius = taps_x.shape[1] // 2
    planes = planes_of(block_x, radius)
    extended_x = block_x + 2 * radius
    vmem = pl.BlockSpec(memory_space=pltpu.VMEM)
    bf16 = jnp.bfloat16
    f32 = jnp.float32
    repeats = ITERS - 1
    return pl.pallas_call(
        functools.partial(sweep_kernel, sizes),
        out_shape=jax.ShapeDtypeStruct(initial.shape, f32),
        in_specs=[pl.BlockSpec(memory_space=pltpu.SMEM)] + [vmem] * 8,
        out_specs=vmem,
        scratch_shapes=[
            pltpu.VMEM((repeats,) + scratch.shape, scratch.dtype)
            for scratch in estimate_scratch(planes, block_x, block_y, depth)
        ]
        + [
            pltpu.VMEM((views, planes, block_y, depth), f32),
            pltpu.VMEM((views, planes + 2 * radius, block_y, depth), f32),
            pltpu.VMEM((ITERS, planes, block_y, depth), f32),
            pltpu.VMEM((ITERS, 2, radius, block_y, depth), bf16),
            pltpu.VMEM((ITERS, 2, planes, HALO_Y, depth), bf16),
            pltpu.VMEM((ITERS, 2, radius, block_y, depth), bf16),
            pltpu.VMEM((ITERS, 2, extended_x, HALO_Y, depth), bf16),
            pltpu.VMEM((ITERS, 2, radius, block_y, depth), bf16),
            pltpu.VMEM((ITERS, 2, extended_x, HALO_Y, depth), bf16),
            pltpu.VMEM((ITERS, planes, block_y, depth), f32),
            pltpu.SemaphoreType.DMA((repeats, 8)),
            pltpu.SemaphoreType.DMA((repeats, 8)),
            pltpu.SemaphoreType.DMA((ITERS, 8)),
            pltpu.SemaphoreType.DMA((ITERS, 8)),
            pltpu.SemaphoreType.DMA((ITERS,)),
            pltpu.SemaphoreType.DMA((ITERS,)),
            pltpu.SemaphoreType.DMA((ITERS, 2)),
            pltpu.SemaphoreType.DMA((ITERS, 2)),
        ],
        compiler_params=pltpu.CompilerParams(
            collective_id=1, has_side_effects=True, vmem_limit_bytes=40 << 20
        ),
    )(taps_x, observed, spreads, initial, inverse_norm, along_y, back_y, along_z, back_z)


def shards(tiles, tile_block, tile_x, tile_y, psf, initial):
    column_count = lax.axis_size("gx")
    column_index = lax.axis_index("gx")
    row_index = lax.axis_index("gy")
    core_index = lax.axis_index("vert")
    local_views = tiles.shape[0]
    all_views = psf.shape[0]
    per_device = tiles.shape[2]
    tile_wide = tiles.shape[3]
    tile_tall = tiles.shape[4]
    block_x, block_y, depth = initial.shape
    capacity = max(2, 2 * per_device // column_count)
    radius = psf.shape[2] // 2
    first_view = core_index * local_views
    mine_psf = lax.dynamic_slice_in_dim(psf, first_view, local_views, 0)

    def my_rows(table):
        chosen = lax.dynamic_slice_in_dim(table, first_view, local_views, 0)
        chosen = lax.dynamic_slice_in_dim(chosen, row_index, 1, 1)[:, 0]
        return chosen.reshape(local_views, column_count, per_device)

    targets = my_rows(tile_block[:, :, :, 0])
    offsets_x = my_rows(tile_x)
    offsets_y = my_rows(tile_y)
    columns_iota = jnp.arange(column_count, dtype=jnp.int32)
    hits = (targets[..., None] == columns_iota).astype(jnp.int32)
    ranks = jnp.cumsum(hits, axis=2, dtype=jnp.int32)
    slot_ids = jnp.arange(capacity, dtype=jnp.int32) + 1
    sent_hits = jnp.swapaxes(lax.dynamic_slice_in_dim(hits, column_index, 1, 1)[:, 0], 1, 2)
    sent_ranks = jnp.swapaxes(lax.dynamic_slice_in_dim(ranks, column_index, 1, 1)[:, 0], 1, 2)
    chooser = sent_hits[:, :, None, :] * (
        sent_ranks[:, :, None, :] == slot_ids[None, None, :, None]
    ).astype(jnp.int32)
    outgoing = jnp.einsum(
        "vgkj,vjabz->gvkabz",
        chooser.astype(jnp.bfloat16),
        tiles[:, 0],
        preferred_element_type=jnp.bfloat16,
    )
    sizes = (column_count, lax.axis_size("gy"))
    halos = first_halos(sizes, radius, initial)
    outgoing, halos = lax.optimization_barrier((outgoing, halos))
    arrived = lax.all_to_all(outgoing, "gx", split_axis=0, concat_axis=0, tiled=True)
    from_hits = lax.dynamic_slice_in_dim(hits, column_index, 1, 3)[..., 0]
    from_ranks = lax.dynamic_slice_in_dim(ranks, column_index, 1, 3)[..., 0]
    picks = from_hits[:, :, None, :] * (
        from_ranks[:, :, None, :] == slot_ids[None, None, :, None]
    ).astype(jnp.int32)
    filled = jnp.sum(picks, axis=3).reshape(local_views, -1)
    corner_x = jnp.sum(picks * offsets_x[:, :, None, :], axis=3).reshape(local_views, -1)
    corner_y = jnp.sum(picks * offsets_y[:, :, None, :], axis=3).reshape(local_views, -1)

    row_iota = jnp.arange(tile_block.shape[1], dtype=jnp.int32)
    global_x = (tile_block[..., 0] * block_x + tile_x).reshape(all_views, -1)
    global_y = (row_iota[None, :, None] * block_y + tile_y).reshape(all_views, -1)
    near_x = jnp.arange(block_x + 2 * radius, dtype=jnp.int32) - radius
    near_y = jnp.arange(block_y + 2 * radius, dtype=jnp.int32) - radius
    cells_x = column_index * block_x + near_x
    cells_y = row_index * block_y + near_y
    cover_x = (
        (cells_x >= global_x[..., None]) & (cells_x < global_x[..., None] + tile_wide)
    ).astype(jnp.bfloat16)
    cover_y = (
        (cells_y >= global_y[..., None]) & (cells_y < global_y[..., None] + tile_tall)
    ).astype(jnp.bfloat16)
    counts = jnp.einsum("vti,vtj->vij", cover_x, cover_y, preferred_element_type=jnp.float32)
    coverage = jnp.minimum(counts, 1.0)
    iota_x = jnp.arange(block_x, dtype=jnp.int32)
    iota_y = jnp.arange(block_y, dtype=jnp.int32)
    iota_z = jnp.arange(depth, dtype=jnp.int32)
    adjoint_x = banded(psf[:, 0], iota_x[:, None] - near_x[None, :] + radius)
    adjoint_y = banded(psf[:, 1], iota_y[:, None] - near_y[None, :] + radius)
    exact = lax.Precision.HIGHEST
    spread = jnp.einsum("vij,vyj->viy", coverage, adjoint_y, precision=exact)
    spread = jnp.einsum("vxi,viy->vxy", adjoint_x, spread, precision=exact)
    profile = jnp.sum(banded(psf[:, 2], iota_z[:, None] - iota_z[None, :] + radius), axis=2)
    norm_field = jnp.einsum("vxy,vz->xyz", spread, profile, precision=exact)
    inverse_norm = 1.0 / (norm_field + damping)

    places_y = jnp.concatenate(
        [
            iota_y,
            jnp.arange(HALO_Y, dtype=jnp.int32) - HALO_Y,
            jnp.arange(HALO_Y, dtype=jnp.int32) + block_y,
        ]
    )
    band_y = banded(mine_psf[:, 1], places_y[None, :] - iota_y[:, None] + radius)
    high, low = split_high_low(band_y)
    flat = (local_views * block_y, places_y.shape[0])
    along_y = jnp.concatenate([high.reshape(flat), low.reshape(flat)], axis=1)
    back_y = jnp.concatenate([high.reshape(flat).T, low.reshape(flat).T], axis=0)
    band_z = banded(mine_psf[:, 2], iota_z[:, None] - iota_z[None, :] + radius)
    along_z = jnp.concatenate(split_high_low(band_z), axis=1)
    back_z = jnp.concatenate(split_high_low(jnp.swapaxes(band_z, 1, 2)), axis=1)
    taps_x = mine_psf[:, 0]
    blurred = first_blur(taps_x, halos, along_y, along_z, block_x)
    observed, spreads = place(filled, corner_x, corner_y, arrived, blurred, back_z, radius)
    return sweeps(
        sizes,
        taps_x,
        observed,
        spreads,
        initial,
        inverse_norm,
        along_y,
        back_y,
        along_z,
        back_z,
    )


def solution(mesh):
    in_specs = (
        P("vert", "gy", ("groups", "gx"), None, None, None),
        P(None, None, "groups", None),
        P(None, None, "groups"),
        P(None, None, "groups"),
        P(),
        P(("groups", "gx"), "gy", None),
    )
    out_specs = P(("groups", "gx"), "gy", None)
    return jax.shard_map(shards, mesh=mesh, in_specs=in_specs, out_specs=out_specs, check_vma=False)
```
